512 devices in a mesh: dp: 32 (over x, y, core), tok: 16 (over z).
Axes of the slice: x: 4, y: 4, z: 16, core: 2. Of those that a mesh axis runs over, the one named last changes fastest.
Arguments:
- student_hidden: bfloat16 [64, 1024, 2048], P('dp', 'tok'), may hold values from -48 to 48
- teacher_values: bfloat16 [64, 1024, 4096], P('dp', 'tok'), may hold values from -48 to 48
- value_weight: bfloat16 [2048, 2048], P(None, 'tok'), may hold values from -0.09375 to 0.09375
- value_bias: bfloat16 [1, 2048], P(None, 'tok'), may hold values from -3 to 3
Outputs:
- hidden_grad: bfloat16 [64, 1024, 2048], P('dp', 'tok')
- bias_grad: float32 [2048], P('tok')
The draws below stay inside these ranges and needn't reach their ends.
All inputs are finite; a program needn't handle non-finite values.
Results may differ from the reference program's by a relative error of at most 0.012.
The reference program's roundings to bfloat16 on the way (of `student_values`, `score_grad` and `value_grad`) count: a program that leaves them out, or rounds other values in their place, can miss the bound.
Values may be sent and summed in bfloat16 or wider, within the bound.
No kernel may reach another device: no remote copies, remote signals or barrier semaphores. Data moves between devices by JAX's collectives and lax.ppermute only.
A program may use at most 64 MiB of HBM per device.

```python
import jax
import jax.numpy as jnp
from jax import lax

DS = 2048
HEADS = 32
SH = 64
TH = 128
LENGTH = 1024
DV = 2048
TW = 4096
SEQS = 64


def shaped_rows(key, width, base_scale):
    first = jax.random.fold_in(key, 0)
    base = jax.random.normal(first, (SEQS, LENGTH, width), jnp.float32)
    return jnp.clip(base_scale * base, -48.0, 48.0)


def draw_student_hidden(key, part):
    return shaped_rows(jax.random.fold_in(key, 11), DS, 1.0).astype(jnp.bfloat16)


def draw_teacher_values(key, part):
    return shaped_rows(jax.random.fold_in(key, 23), TW, 0.7).astype(jnp.bfloat16)


def block_scale(stream_key, extent, cuts, low, high):
    def one(axis_at, blocks):
        heights = jax.random.uniform(jax.random.fold_in(jax.random.fold_in(stream_key, 6), axis_at), (blocks,), jnp.float32, low / len(cuts), high / len(cuts))
        return jnp.repeat(jnp.exp(heights), extent[axis_at] // blocks).reshape((-1,) + (1,) * (len(extent) - axis_at - 1))

    loudness = one(*cuts[0])
    for cut in cuts[1:]:
        loudness = loudness * one(*cut)
    return loudness


def bell_draw(key, dims, deviation, bound, cuts=(), held_as=jnp.bfloat16):
    values = deviation * jax.random.normal(key, dims, jnp.float32)
    if cuts:
        values = values * block_scale(key, dims, cuts, -0.22, 0.18)
    return jnp.clip(values, -bound, bound).astype(held_as)


def setup_inputs(seed: int = 0) -> dict:
    splits = jax.random.split(jax.random.key(seed), 5)
    return {
        "student_hidden": draw_student_hidden(jax.random.fold_in(splits[4], 71), 0),
        "teacher_values": draw_teacher_values(jax.random.fold_in(splits[4], 71), 0),
        "value_weight": bell_draw(splits[2], (DS, DV), (2 * DS) ** -0.5, 0.09375, ((1, 16),)),
        "value_bias": bell_draw(splits[3], (1, DV), 0.5, 3.0, ((1, 16),)),
    }


def head_grads(student_head, teacher_head):
    teacher_scores = jnp.dot(teacher_head, teacher_head.T, preferred_element_type=jnp.float32) / jnp.sqrt(jnp.float32(TH))
    teacher_prob = jax.nn.softmax(teacher_scores, axis=-1)
    student_scores = jnp.dot(student_head, student_head.T, preferred_element_type=jnp.float32) / jnp.sqrt(jnp.float32(SH))
    student_prob = jax.nn.softmax(student_scores, axis=-1)
    score_grad = (LENGTH * (student_prob - teacher_prob)).astype(jnp.bfloat16)
    summed = jnp.dot(score_grad, student_head, preferred_element_type=jnp.float32) + jnp.dot(score_grad.T, student_head, preferred_element_type=jnp.float32)
    return (summed / jnp.sqrt(jnp.float32(SH))).astype(jnp.bfloat16)

def reference(student_hidden, teacher_values, value_weight, value_bias):
    rows = student_hidden.reshape(SEQS * LENGTH, DS)
    student_values = (jnp.dot(rows, value_weight, preferred_element_type=jnp.float32) + value_bias.astype(jnp.float32)).astype(jnp.bfloat16)
    student_items = student_values.reshape(SEQS, LENGTH, HEADS, SH).transpose(0, 2, 1, 3).reshape(SEQS * HEADS, LENGTH, SH)
    teacher_items = teacher_values.reshape(SEQS, LENGTH, HEADS, TH).transpose(0, 2, 1, 3).reshape(SEQS * HEADS, LENGTH, TH)
    grads = lax.map(lambda pair: head_grads(pair[0], pair[1]), (student_items, teacher_items))
    value_grad = grads.reshape(SEQS, HEADS, LENGTH, SH).transpose(0, 2, 1, 3).reshape(SEQS * LENGTH, DV)
    hidden_grad = jnp.dot(value_grad, value_weight.T, preferred_element_type=jnp.float32).astype(jnp.bfloat16)
    bias_grad = lax.optimization_barrier(jnp.sum(value_grad.astype(jnp.float32), axis=0)) / jnp.sqrt(jnp.float32(SEQS * LENGTH))
    return (hidden_grad.reshape(SEQS, LENGTH, DS), bias_grad)
```

```python
import functools
import math

import jax
import jax.numpy as jnp
from jax import lax
from jax.experimental import pallas as pl
from jax.experimental.pallas import tpu as pltpu
from jax.sharding import PartitionSpec as P

SH = 64
TH = 128
LOG2E = 1.4426950408889634
NT = (((1,), (1,)), ((), ()))
TN = (((0,), (0,)), ((), ()))
NN = (((1,), (0,)), ((), ()))
F32 = jnp.float32
BF16 = jnp.bfloat16


def dot(a, b, dims):
    return lax.dot_general(a, b, dims, preferred_element_type=F32)


def params(mib):
    return pltpu.CompilerParams(vmem_limit_bytes=mib << 20)


def split_columns(x, parts):
    rows, width = x.shape
    cols = width // parts

    def kernel(x_ref, o_ref):
        o_ref[0] = x_ref[...]

    return pl.pallas_call(
        kernel,
        grid=(parts,),
        in_specs=[pl.BlockSpec((rows, cols), lambda t: (0, t))],
        out_specs=pl.BlockSpec((1, rows, cols), lambda t: (t, 0, 0)),
        out_shape=jax.ShapeDtypeStruct((parts, rows, cols), x.dtype),
        name="split_columns",
    )(x)


def project(hidden, weight, bias):
    seqs, toks, width = hidden.shape
    groups, blocks, depth, cols = weight.shape
    pair = 2

    def kernel(h_ref, w_ref, b_ref, *outs):
        h = h_ref[...].reshape(seqs * toks, width)
        w = jnp.concatenate(
            [w_ref[:, k].reshape(groups * depth, cols) for k in range(pair)], axis=1
        )
        r = dot(h, w, NN)
        for k in range(pair):
            v = (r[:, k * cols : (k + 1) * cols] + b_ref[k].astype(F32)).astype(BF16)
            for s in range(seqs):
                outs[s][k] = v[s * toks : (s + 1) * toks]

    return pl.pallas_call(
        kernel,
        grid=(blocks // pair,),
        in_specs=[
            pl.BlockSpec((seqs, toks, width), lambda t: (0, 0, 0)),
            pl.BlockSpec((groups, pair, depth, cols), lambda t: (0, t, 0, 0)),
            pl.BlockSpec((pair, 1, cols), lambda t: (t, 0, 0)),
        ],
        out_specs=[pl.BlockSpec((pair, toks, cols), lambda t: (t, 0, 0))] * seqs,
        out_shape=[jax.ShapeDtypeStruct((blocks, toks, cols), BF16)] * seqs,
        compiler_params=params(32),
        cost_estimate=pl.CostEstimate(
            flops=2 * seqs * toks * width * blocks * cols,
            bytes_accessed=2 * width * blocks * cols,
            transcendentals=0,
        ),
        name="project",
    )(hidden, weight, bias)


def soft(scores, scale, total):
    peak = jnp.max(scores, axis=1, keepdims=True)
    e = jnp.exp2((scores - peak) * scale)
    return e * (total / jnp.sum(e, axis=1, keepdims=True))


def teacher_probs(teacher, seqs):
    blocks, rows, width = teacher.shape
    toks = rows // seqs
    length = blocks * toks
    heads = width // TH
    step = 256
    t4 = teacher.reshape(blocks, seqs, toks, width)

    def kernel(t_ref, o_ref):
        i = pl.program_id(2)
        part = step // toks
        t = t_ref[...].reshape(length, TH)
        q = t_ref[pl.ds(i * part, part)].reshape(step, TH)
        o_ref[0, 0] = soft(dot(q, t, NT), LOG2E / math.sqrt(TH), float(length))

    return pl.pallas_call(
        kernel,
        grid=(seqs, heads, length // step),
        in_specs=[
            pl.BlockSpec((blocks, None, toks, TH), lambda s, h, i: (0, s, 0, h))
        ],
        out_specs=pl.BlockSpec((1, 1, step, length), lambda s, h, i: (s, h, i, 0)),
        out_shape=jax.ShapeDtypeStruct((seqs, heads, length, length), F32),
        compiler_params=params(40),
        cost_estimate=pl.CostEstimate(
            flops=2 * seqs * heads * length * length * TH,
            bytes_accessed=4 * seqs * heads * length * length,
            transcendentals=seqs * heads * length * length,
        ),
        name="teacher_probs",
    )(t4)


def head_grads(student, probs, seq):
    blocks, toks, cols = student.shape
    length = blocks * toks
    heads = cols // SH
    step = 256
    part = step // toks
    last = length // step - 1

    def kernel(s_ref, p_ref, o_ref, b_ref, rows, trans):
        i = pl.program_id(0)
        s = s_ref[...].reshape(length, cols)
        q = s_ref[pl.ds(i * part, part)].reshape(step, cols)
        lane = lax.broadcasted_iota(jnp.int32, (step, cols), 1) // SH
        here = jnp.zeros((step, cols), F32)
        across = jnp.zeros((cols, length), F32)
        for h in range(heads):
            qh = jnp.where(lane == h, q, jnp.zeros_like(q))
            p = soft(dot(qh, s, NT), LOG2E / math.sqrt(SH), float(length))
            g = (p - p_ref[0, h]).astype(BF16)
            here = jnp.where(lane == h, dot(g, s, NN), here)
            across = across + dot(qh, g, TN)
        rows[pl.ds(i * step, step)] = here

        @pl.when(i == 0)
        def _():
            trans[...] = across

        @pl.when(i > 0)
        def _():
            trans[...] += across

        @pl.when(i == last)
        def _():
            grad = ((rows[...] + trans[...].T) * (1.0 / math.sqrt(SH))).astype(BF16)
            o_ref[...] = grad.reshape(blocks, toks, cols)
            b_ref[...] = jnp.sum(grad.astype(F32), axis=0, keepdims=True)

    return pl.pallas_call(
        kernel,
        grid=(length // step,),
        in_specs=[
            pl.BlockSpec((blocks, toks, cols), lambda i: (0, 0, 0)),
            pl.BlockSpec((1, heads, step, length), lambda i: (seq, 0, i, 0)),
        ],
        out_specs=[
            pl.BlockSpec((blocks, toks, cols), lambda i: (0, 0, 0)),
            pl.BlockSpec((1, cols), lambda i: (0, 0)),
        ],
        out_shape=[
            jax.ShapeDtypeStruct((blocks, toks, cols), BF16),
            jax.ShapeDtypeStruct((1, cols), F32),
        ],
        scratch_shapes=[pltpu.VMEM((length, cols), F32), pltpu.VMEM((cols, length), F32)],
        compiler_params=params(48),
        cost_estimate=pl.CostEstimate(
            flops=6 * heads * length * length * cols,
            bytes_accessed=4 * heads * length * length,
            transcendentals=heads * length * length,
        ),
        name="head_grads",
    )(student, probs)


def hidden_grads(grads, weight):
    seqs = len(grads)
    blocks, toks, cols = grads[0].shape
    groups, _, depth, _ = weight.shape
    take = max(1, 256 // depth)

    def kernel(*refs):
        w_ref, o_ref = refs[seqs], refs[seqs + 1]
        acc = jnp.zeros((seqs * toks, take * depth), F32)
        for t in range(0, blocks, 2):
            g = jnp.concatenate(
                [
                    jnp.concatenate([refs[s][t + k] for k in range(2)], axis=1)
                    for s in range(seqs)
                ],
                axis=0,
            )
            w = jnp.concatenate(
                [w_ref[:, t + k].reshape(take * depth, cols) for k in range(2)], axis=1
            )
            acc = acc + dot(g, w, NT)
        o_ref[...] = acc.astype(BF16).reshape(seqs, toks, take * depth)

    return pl.pallas_call(
        kernel,
        grid=(groups // take,),
        in_specs=[pl.BlockSpec((blocks, toks, cols), lambda n: (0, 0, 0))] * seqs
        + [pl.BlockSpec((take, blocks, depth, cols), lambda n: (n, 0, 0, 0))],
        out_specs=pl.BlockSpec((seqs, toks, take * depth), lambda n: (0, 0, n)),
        out_shape=jax.ShapeDtypeStruct((seqs, toks, groups * depth), BF16),
        compiler_params=params(32),
        cost_estimate=pl.CostEstimate(
            flops=2 * seqs * toks * groups * depth * blocks * cols,
            bytes_accessed=2 * groups * depth * blocks * cols,
            transcendentals=0,
        ),
        name="hidden_grads",
    )(*grads, weight)


def sum_over(x, axis):
    size = lax.axis_size(axis)
    reach = 1
    while reach < size:
        x = x + lax.ppermute(x, axis, [(i, i ^ reach) for i in range(size)])
        reach *= 2
    return x


def exchange(x):
    return lax.all_to_all(x, "tok", split_axis=0, concat_axis=0, tiled=True)


def body(student_hidden, teacher_values, value_weight, value_bias):
    seqs, toks, width = student_hidden.shape
    groups, parts = lax.axis_size("dp"), lax.axis_size("tok")
    cols = value_weight.shape[1]
    depth = width // groups

    piece = lax.dynamic_slice_in_dim(value_weight, lax.axis_index("dp") * depth, depth)
    piece = jnp.concatenate([piece, jnp.broadcast_to(value_bias, (8, cols))], axis=0)
    pieces = exchange(jnp.broadcast_to(piece, (parts, depth + 8, cols)))
    weight = lax.all_gather(pieces[:, :depth], "dp", axis=0, tiled=False)
    bias = pieces[:, depth : depth + 1]

    teacher = exchange(
        split_columns(teacher_values.reshape(seqs * toks, -1), parts)
    )
    probs = teacher_probs(teacher, seqs)

    values = [exchange(v) for v in project(student_hidden, weight, bias)]
    grads, sums = [], []
    for s in range(seqs):
        grad, total = head_grads(values[s], probs, s)
        grads.append(exchange(grad))
        sums.append(total)
    hidden_grad = hidden_grads(grads, weight)
    tokens = seqs * toks * parts * groups
    bias_grad = sum_over(sum(sums[1:], sums[0]), "dp")[0] / math.sqrt(tokens)
    return (hidden_grad, bias_grad)


def solution(mesh):
    placed = (P("dp", "tok", None), P("dp", "tok", None), P(None, "tok"), P(None, "tok"))
    return jax.shard_map(
        body,
        mesh=mesh,
        in_specs=placed,
        out_specs=(P("dp", "tok", None), P("tok")),
        check_vma=False,
    )
```

```python
import math

import jax
import jax.numpy as jnp
from jax import lax
from jax.experimental import pallas as pl
from jax.experimental.pallas import tpu as pltpu
from jax.sharding import PartitionSpec as P


SH = 64
TH = 128
LOG2E = 1.4426950408889634
NT = (((1,), (1,)), ((), ()))
TN = (((0,), (0,)), ((), ()))
NN = (((1,), (0,)), ((), ()))
F32 = jnp.float32
BF16 = jnp.bfloat16


def dot(a, b, dims):
    return lax.dot_general(a, b, dims, preferred_element_type=F32)


def params(mib):
    return pltpu.CompilerParams(vmem_limit_bytes=mib << 20)


def split_columns(x, parts):
    rows, width = x.shape
    cols = width // parts

    def kernel(x_ref, o_ref):
        o_ref[0] = x_ref[...]

    return pl.pallas_call(
        kernel,
        grid=(parts,),
        in_specs=[pl.BlockSpec((rows, cols), lambda t: (0, t))],
        out_specs=pl.BlockSpec((1, rows, cols), lambda t: (t, 0, 0)),
        out_shape=jax.ShapeDtypeStruct((parts, rows, cols), x.dtype),
        name="split_columns",
    )(x)


SIDE = 4
LANE = 128


def ring_pairs(shift, first):
    def place(x, y, c):
        return ((x % SIDE) * SIDE + y % SIDE) * 2 + c

    pairs = []
    for x in range(SIDE):
        for y in range(SIDE):
            for c in range(2):
                dx, dy = (shift, 0) if (c == 0) == first else (0, shift)
                pairs.append((place(x, y, c), place(x + dx, y + dy, c)))
    return pairs


def gather_weight(piece):
    def send(v, shift, first):
        return lax.ppermute(v, "dp", ring_pairs(shift, first))

    near = [send(piece, k, True) for k in (1, -1, 2)]
    own = jnp.stack([piece, near[0], near[2], near[1]])
    down, up = send(own, 1, False), send(own, -1, False)
    half = SIDE // 2
    low, high = send(down[:half], 1, False), send(up[half:], -1, False)
    mine = [own, down, low, high, up]
    swap = [(d, d ^ 1) for d in range(2 * SIDE * SIDE)]
    theirs = [lax.ppermute(v, "dp", swap) for v in mine]
    return mine + theirs


def blocks_of():
    table = []
    for d in range(2 * SIDE * SIDE):
        x, y, c = d // (2 * SIDE), d // 2 % SIDE, d % 2
        table.append(
            [(x - j) % SIDE * SIDE + (y - b) % SIDE for j in range(SIDE) for b in range(SIDE)]
            + [c]
        )
    return lax.dynamic_index_in_dim(
        jnp.array(table, jnp.int32), lax.axis_index("dp"), keepdims=False
    )


def weight_block(refs, core, k):
    def pick(side, b, j):
        part = refs[5 * side : 5 * side + 5]
        if b == 2:
            half = SIDE // 2
            return part[2 + j // half][j % half, k]
        return part[{0: 0, 1: 1, 3: 4}[b]][j, k]

    rows = []
    for j in range(SIDE):
        for b in range(SIDE):
            rows.append(jnp.where(core == 0, pick(0, b, j), pick(1, b, j)))
            rows.append(jnp.where(core == 0, pick(1, j, b), pick(0, j, b)))
    return jnp.concatenate(rows, axis=0)


def weight_specs(weights, pair):
    return [
        pl.BlockSpec((w.shape[0], pair) + w.shape[2:], lambda t, place: (0, t, 0, 0))
        for w in weights
    ]


def project(hidden, weights, bias, place):
    rows, width = hidden.shape
    blocks, cols = weights[0].shape[1], weights[0].shape[3]
    pair = 2
    count = len(weights)

    def kernel(place_ref, h_ref, b_ref, *refs):
        w_refs, o_ref, h = refs[:count], refs[count], refs[count + 1]

        @pl.when(pl.program_id(0) == 0)
        def _():
            for m in range(width // LANE):
                at = pl.multiple_of(place_ref[m] * LANE, LANE)
                h[:, m * LANE : (m + 1) * LANE] = h_ref[:, pl.ds(at, LANE)]

        core = place_ref[width // LANE]
        w = jnp.concatenate(
            [weight_block(w_refs, core, k) for k in range(pair)], axis=1
        )
        r = dot(h[...], w, NN)
        for k in range(pair):
            o_ref[k] = (r[:, k * cols : (k + 1) * cols] + b_ref[k].astype(F32)).astype(BF16)

    return pl.pallas_call(
        kernel,
        grid_spec=pltpu.PrefetchScalarGridSpec(
            num_scalar_prefetch=1,
            grid=(blocks // pair,),
            in_specs=[
                pl.BlockSpec((rows, width), lambda t, place: (0, 0)),
                pl.BlockSpec((pair, 1, cols), lambda t, place: (t, 0, 0)),
            ]
            + weight_specs(weights, pair),
            out_specs=pl.BlockSpec((pair, rows, cols), lambda t, place: (t, 0, 0)),
            scratch_shapes=[pltpu.VMEM((rows, width), BF16)],
        ),
        out_shape=jax.ShapeDtypeStruct((blocks, rows, cols), BF16),
        compiler_params=params(32),
        cost_estimate=pl.CostEstimate(
            flops=2 * rows * width * blocks * cols,
            bytes_accessed=2 * width * blocks * cols,
            transcendentals=0,
        ),
        name="project",
    )(place, hidden, bias, *weights)


def soft(scores, scale, total):
    peak = jnp.max(scores, axis=1, keepdims=True)
    e = jnp.exp2((scores - peak) * scale)
    return e * (total / jnp.sum(e, axis=1, keepdims=True))


def teacher_probs(teacher, seqs):
    blocks, rows, width = teacher.shape
    toks = rows // seqs
    length = blocks * toks
    heads = width // TH
    step = 256
    t4 = teacher.reshape(blocks, seqs, toks, width)

    def kernel(t_ref, o_ref):
        i = pl.program_id(2)
        part = step // toks
        t = t_ref[...].reshape(length, TH)
        q = t_ref[pl.ds(i * part, part)].reshape(step, TH)
        o_ref[0, 0] = soft(dot(q, t, NT), LOG2E / math.sqrt(TH), float(length))

    return pl.pallas_call(
        kernel,
        grid=(seqs, heads, length // step),
        in_specs=[
            pl.BlockSpec((blocks, None, toks, TH), lambda s, h, i: (0, s, 0, h))
        ],
        out_specs=pl.BlockSpec((1, 1, step, length), lambda s, h, i: (s, h, i, 0)),
        out_shape=jax.ShapeDtypeStruct((seqs, heads, length, length), F32),
        compiler_params=params(40),
        cost_estimate=pl.CostEstimate(
            flops=2 * seqs * heads * length * length * TH,
            bytes_accessed=4 * seqs * heads * length * length,
            transcendentals=seqs * heads * length * length,
        ),
        name="teacher_probs",
    )(t4)


def head_grads(student, probs):
    seqs = probs.shape[0]
    blocks, both, cols = student.shape
    toks = both // seqs
    length = blocks * toks
    heads = cols // SH
    step = 256
    part = step // toks
    last = length // step - 1

    def kernel(s_ref, p_ref, o_ref, b_ref, rows, trans):
        i = pl.program_id(1)
        s = s_ref[...].reshape(length, cols)
        q = s_ref[pl.ds(i * part, part)].reshape(step, cols)
        lane = lax.broadcasted_iota(jnp.int32, (step, cols), 1) // SH
        here = jnp.zeros((step, cols), F32)
        across = jnp.zeros((cols, length), F32)
        for h in range(heads):
            qh = jnp.where(lane == h, q, jnp.zeros_like(q))
            p = soft(dot(qh, s, NT), LOG2E / math.sqrt(SH), float(length))
            g = (p - p_ref[0, h]).astype(BF16)
            here = jnp.where(lane == h, dot(g, s, NN), here)
            across = across + dot(qh, g, TN)
        rows[pl.ds(i * step, step)] = here

        @pl.when(i == 0)
        def _():
            trans[...] = across

        @pl.when(i > 0)
        def _():
            trans[...] += across

        @pl.when(i == last)
        def _():
            grad = ((rows[...] + trans[...].T) * (1.0 / math.sqrt(SH))).astype(BF16)
            o_ref[...] = grad.reshape(blocks, toks, cols)
            total = jnp.sum(grad.astype(F32), axis=0, keepdims=True)
            b_ref[...] = jnp.where(pl.program_id(0) == 0, total, b_ref[...] + total)

    grads, total = pl.pallas_call(
        kernel,
        grid=(seqs, length // step),
        in_specs=[
            pl.BlockSpec((blocks, None, toks, cols), lambda s, i: (0, s, 0, 0)),
            pl.BlockSpec((1, heads, step, length), lambda s, i: (s, 0, i, 0)),
        ],
        out_specs=[
            pl.BlockSpec((blocks, None, toks, cols), lambda s, i: (0, s, 0, 0)),
            pl.BlockSpec((1, cols), lambda s, i: (0, 0)),
        ],
        out_shape=[
            jax.ShapeDtypeStruct((blocks, seqs, toks, cols), BF16),
            jax.ShapeDtypeStruct((1, cols), F32),
        ],
        scratch_shapes=[pltpu.VMEM((length, cols), F32), pltpu.VMEM((cols, length), F32)],
        compiler_params=params(48),
        cost_estimate=pl.CostEstimate(
            flops=6 * seqs * heads * length * length * cols,
            bytes_accessed=4 * seqs * heads * length * length,
            transcendentals=seqs * heads * length * length,
        ),
        name="head_grads",
    )(student.reshape(blocks, seqs, toks, cols), probs)
    return grads.reshape(student.shape), total


def hidden_grads(grads, weights, place):
    blocks, rows, cols = grads.shape
    width = weights[0].shape[2] * 2 * SIDE * SIDE
    pair = 2
    count = len(weights)
    last = blocks // pair - 1

    def kernel(place_ref, g_ref, *refs):
        w_refs, o_ref, acc = refs[:count], refs[count], refs[count + 1]
        t = pl.program_id(0)
        core = place_ref[width // LANE]
        w = jnp.concatenate(
            [weight_block(w_refs, core, k) for k in range(pair)], axis=1
        )
        g = jnp.concatenate([g_ref[k] for k in range(pair)], axis=1)
        r = dot(g, w, NT)

        @pl.when(t == 0)
        def _():
            acc[...] = r

        @pl.when(t > 0)
        def _():
            acc[...] += r

        @pl.when(t == last)
        def _():
            for m in range(width // LANE):
                at = pl.multiple_of(place_ref[m] * LANE, LANE)
                o_ref[:, pl.ds(at, LANE)] = acc[:, m * LANE : (m + 1) * LANE].astype(BF16)

    return pl.pallas_call(
        kernel,
        grid_spec=pltpu.PrefetchScalarGridSpec(
            num_scalar_prefetch=1,
            grid=(blocks // pair,),
            in_specs=[pl.BlockSpec((pair, rows, cols), lambda t, place: (t, 0, 0))]
            + weight_specs(weights, pair),
            out_specs=pl.BlockSpec((rows, width), lambda t, place: (0, 0)),
            scratch_shapes=[pltpu.VMEM((rows, width), F32)],
        ),
        out_shape=jax.ShapeDtypeStruct((rows, width), BF16),
        compiler_params=params(32),
        cost_estimate=pl.CostEstimate(
            flops=2 * rows * width * blocks * cols,
            bytes_accessed=2 * width * blocks * cols,
            transcendentals=0,
        ),
        name="hidden_grads",
    )(place, grads, *weights)


def sum_over(x, axis):
    size = lax.axis_size(axis)
    reach = 1
    while reach < size:
        x = x + lax.ppermute(x, axis, [(i, i ^ reach) for i in range(size)])
        reach *= 2
    return x


def exchange(x):
    return lax.all_to_all(x, "tok", split_axis=0, concat_axis=0, tiled=True)


def body(student_hidden, teacher_values, value_weight, value_bias):
    seqs, toks, width = student_hidden.shape
    groups, parts = lax.axis_size("dp"), lax.axis_size("tok")
    cols = value_weight.shape[1]
    depth = width // groups

    piece = lax.dynamic_slice_in_dim(value_weight, lax.axis_index("dp") * depth, depth)
    piece = jnp.concatenate([piece, jnp.broadcast_to(value_bias, (8, cols))], axis=0)
    pieces = exchange(jnp.broadcast_to(piece, (parts, depth + 8, cols)))
    bias = pieces[:, depth : depth + 1]

    columns = split_columns(teacher_values.reshape(seqs * toks, -1), parts)
    teacher = exchange(columns)
    weights = gather_weight(pieces[:, :depth])
    probs = teacher_probs(teacher, seqs)

    place = blocks_of()
    rows = student_hidden.reshape(seqs * toks, width)
    values = project(rows, weights, bias, place)
    values = exchange(values)
    grads, total = head_grads(values, probs)
    grads = exchange(grads)
    hidden_grad = hidden_grads(grads, weights, place).reshape(student_hidden.shape)
    tokens = seqs * toks * parts * groups
    bias_grad = sum_over(total, "dp")[0] / math.sqrt(tokens)
    return (hidden_grad, bias_grad)


def solution(mesh):
    placed = (P("dp", "tok", None), P("dp", "tok", None), P(None, "tok"), P(None, "tok"))
    return jax.shard_map(
        body,
        mesh=mesh,
        in_specs=placed,
        out_specs=(P("dp", "tok", None), P("tok")),
        check_vma=False,
    )
```

```python
import math

import jax
import jax.numpy as jnp
from jax import lax
from jax.experimental import pallas as pl
from jax.experimental.pallas import tpu as pltpu
from jax.sharding import PartitionSpec as P


SH = 64
TH = 128
LOG2E = 1.4426950408889634
NT = (((1,), (1,)), ((), ()))
TN = (((0,), (0,)), ((), ()))
NN = (((1,), (0,)), ((), ()))
F32 = jnp.float32
BF16 = jnp.bfloat16


def dot(a, b, dims):
    return lax.dot_general(a, b, dims, preferred_element_type=F32)


def params(mib):
    return pltpu.CompilerParams(vmem_limit_bytes=mib << 20)


def split_columns(x, parts):
    rows, width = x.shape
    cols = width // parts

    def kernel(x_ref, o_ref):
        o_ref[0] = x_ref[...]

    return pl.pallas_call(
        kernel,
        grid=(parts,),
        in_specs=[pl.BlockSpec((rows, cols), lambda t: (0, t))],
        out_specs=pl.BlockSpec((1, rows, cols), lambda t: (t, 0, 0)),
        out_shape=jax.ShapeDtypeStruct((parts, rows, cols), x.dtype),
        name="split_columns",
    )(x)


SIDE = 4
LANE = 128


def ring_pairs(shift, first):
    def place(x, y, c):
        return ((x % SIDE) * SIDE + y % SIDE) * 2 + c

    pairs = []
    for x in range(SIDE):
        for y in range(SIDE):
            for c in range(2):
                dx, dy = (shift, 0) if (c == 0) == first else (0, shift)
                pairs.append((place(x, y, c), place(x + dx, y + dy, c)))
    return pairs


def gather_weight(piece):
    def send(v, shift, first):
        return lax.ppermute(v, "dp", ring_pairs(shift, first))

    below, above, far = [send(piece, k, True) for k in (1, -1, 2)]
    own = [jnp.stack([piece, below]), jnp.stack([far, above])]
    down0, up1 = send(own[0], 1, False), send(own[1], -1, False)
    down1, up0 = send(own[1], 1, False), send(own[0], -1, False)
    far0, far1 = send(down0, 1, False), send(up1, -1, False)
    swap = [(d, d ^ 1) for d in range(2 * SIDE * SIDE)]
    mine, theirs = [], []
    for parts in (own, [down0, down1], [far0, far1], [up0, up1]):
        theirs += [lax.ppermute(v, "dp", swap) for v in parts]
        mine += parts
    return mine + theirs


def blocks_of():
    table = []
    for d in range(2 * SIDE * SIDE):
        x, y, c = d // (2 * SIDE), d // 2 % SIDE, d % 2
        table.append(
            [(x - j) % SIDE * SIDE + (y - b) % SIDE for j in range(SIDE) for b in range(SIDE)]
            + [c]
        )
    return lax.dynamic_index_in_dim(
        jnp.array(table, jnp.int32), lax.axis_index("dp"), keepdims=False
    )


def weight_block(refs, core, k):
    half = SIDE // 2
    count = len(refs) // 2

    def pick(side, b, j):
        return refs[(side ^ core) * count + 2 * b + j // half][j % half, k]

    rows = []
    for j in range(SIDE):
        for b in range(SIDE):
            rows += [pick(0, b, j), pick(1, j, b)]
    return jnp.concatenate(rows, axis=0)


def on_core(core, step):
    for c in range(2):
        pl.when(core == c)(lambda c=c: step(c))


def weight_specs(weights, pair):
    return [
        pl.BlockSpec((w.shape[0], pair) + w.shape[2:], lambda t, place: (0, t, 0, 0))
        for w in weights
    ]


def project(hidden, weights, bias, place):
    rows, width = hidden.shape
    blocks, cols = weights[0].shape[1], weights[0].shape[3]
    pair = 2
    count = len(weights)

    def kernel(place_ref, h_ref, b_ref, *refs):
        w_refs, o_ref, h = refs[:count], refs[count], refs[count + 1]

        @pl.when(pl.program_id(0) == 0)
        def _():
            for m in range(width // LANE):
                at = pl.multiple_of(place_ref[m] * LANE, LANE)
                h[:, m * LANE : (m + 1) * LANE] = h_ref[:, pl.ds(at, LANE)]

        def step(core):
            w = jnp.concatenate(
                [weight_block(w_refs, core, k) for k in range(pair)], axis=1
            )
            r = dot(h[...], w, NN)
            for k in range(pair):
                v = r[:, k * cols : (k + 1) * cols] + b_ref[k].astype(F32)
                o_ref[k] = v.astype(BF16)

        on_core(place_ref[width // LANE], step)

    return pl.pallas_call(
        kernel,
        grid_spec=pltpu.PrefetchScalarGridSpec(
            num_scalar_prefetch=1,
            grid=(blocks // pair,),
            in_specs=[
                pl.BlockSpec((rows, width), lambda t, place: (0, 0)),
                pl.BlockSpec((pair, 1, cols), lambda t, place: (t, 0, 0)),
            ]
            + weight_specs(weights, pair),
            out_specs=pl.BlockSpec((pair, rows, cols), lambda t, place: (t, 0, 0)),
            scratch_shapes=[pltpu.VMEM((rows, width), BF16)],
        ),
        out_shape=jax.ShapeDtypeStruct((blocks, rows, cols), BF16),
        compiler_params=params(32),
        cost_estimate=pl.CostEstimate(
            flops=2 * rows * width * blocks * cols,
            bytes_accessed=2 * width * blocks * cols,
            transcendentals=0,
        ),
        name="project",
    )(place, hidden, bias, *weights)


def soft(scores, scale, total):
    peak = jnp.max(scores, axis=1, keepdims=True)
    e = jnp.exp2((scores - peak) * scale)
    return e * (total / jnp.sum(e, axis=1, keepdims=True))


def teacher_probs(teacher, seqs):
    blocks, rows, width = teacher.shape
    toks = rows // seqs
    length = blocks * toks
    heads = width // TH
    step = 256
    t4 = teacher.reshape(blocks, seqs, toks, width)

    def kernel(t_ref, o_ref):
        i = pl.program_id(2)
        part = step // toks
        t = t_ref[...].reshape(length, TH)
        q = t_ref[pl.ds(i * part, part)].reshape(step, TH)
        o_ref[0, 0] = soft(dot(q, t, NT), LOG2E / math.sqrt(TH), float(length))

    return pl.pallas_call(
        kernel,
        grid=(seqs, heads, length // step),
        in_specs=[
            pl.BlockSpec((blocks, None, toks, TH), lambda s, h, i: (0, s, 0, h))
        ],
        out_specs=pl.BlockSpec((1, 1, step, length), lambda s, h, i: (s, h, i, 0)),
        out_shape=jax.ShapeDtypeStruct((seqs, heads, length, length), F32),
        compiler_params=params(40),
        cost_estimate=pl.CostEstimate(
            flops=2 * seqs * heads * length * length * TH,
            bytes_accessed=4 * seqs * heads * length * length,
            transcendentals=seqs * heads * length * length,
        ),
        name="teacher_probs",
    )(t4)


def head_grads(student, probs):
    seqs = probs.shape[0]
    blocks, both, cols = student.shape
    toks = both // seqs
    length = blocks * toks
    heads = cols // SH
    step = 256
    part = step // toks
    last = length // step - 1

    def kernel(s_ref, p_ref, o_ref, b_ref, rows, trans):
        i = pl.program_id(1)
        s = s_ref[...].reshape(length, cols)
        q = s_ref[pl.ds(i * part, part)].reshape(step, cols)
        lane = lax.broadcasted_iota(jnp.int32, (step, cols), 1) // SH
        here = jnp.zeros((step, cols), F32)
        across = jnp.zeros((cols, length), F32)
        for h in range(heads):
            qh = jnp.where(lane == h, q, jnp.zeros_like(q))
            p = soft(dot(qh, s, NT), LOG2E / math.sqrt(SH), float(length))
            g = (p - p_ref[0, h]).astype(BF16)
            here = jnp.where(lane == h, dot(g, s, NN), here)
            across = across + dot(qh, g, TN)
        rows[pl.ds(i * step, step)] = here

        @pl.when(i == 0)
        def _():
            trans[...] = across

        @pl.when(i > 0)
        def _():
            trans[...] += across

        @pl.when(i == last)
        def _():
            grad = ((rows[...] + trans[...].T) * (1.0 / math.sqrt(SH))).astype(BF16)
            o_ref[...] = grad.reshape(blocks, toks, cols)
            total = jnp.sum(grad.astype(F32), axis=0, keepdims=True)
            b_ref[...] = jnp.where(pl.program_id(0) == 0, total, b_ref[...] + total)

    grads, total = pl.pallas_call(
        kernel,
        grid=(seqs, length // step),
        in_specs=[
            pl.BlockSpec((blocks, None, toks, cols), lambda s, i: (0, s, 0, 0)),
            pl.BlockSpec((1, heads, step, length), lambda s, i: (s, 0, i, 0)),
        ],
        out_specs=[
            pl.BlockSpec((blocks, None, toks, cols), lambda s, i: (0, s, 0, 0)),
            pl.BlockSpec((1, cols), lambda s, i: (0, 0)),
        ],
        out_shape=[
            jax.ShapeDtypeStruct((blocks, seqs, toks, cols), BF16),
            jax.ShapeDtypeStruct((1, cols), F32),
        ],
        scratch_shapes=[pltpu.VMEM((length, cols), F32), pltpu.VMEM((cols, length), F32)],
        compiler_params=params(48),
        cost_estimate=pl.CostEstimate(
            flops=6 * seqs * heads * length * length * cols,
            bytes_accessed=4 * seqs * heads * length * length,
            transcendentals=seqs * heads * length * length,
        ),
        name="head_grads",
    )(student.reshape(blocks, seqs, toks, cols), probs)
    return grads.reshape(student.shape), total


def hidden_grads(grads, weights, place):
    blocks, rows, cols = grads.shape
    width = weights[0].shape[2] * 2 * SIDE * SIDE
    pair = 2
    count = len(weights)
    last = blocks // pair - 1

    def kernel(place_ref, g_ref, *refs):
        w_refs, o_ref, acc = refs[:count], refs[count], refs[count + 1]
        t = pl.program_id(0)

        @pl.when(t == 0)
        def _():
            acc[...] = jnp.zeros_like(acc)

        def step(core):
            w = jnp.concatenate(
                [weight_block(w_refs, core, k) for k in range(pair)], axis=1
            )
            g = jnp.concatenate([g_ref[k] for k in range(pair)], axis=1)
            acc[...] += dot(g, w, NT)

        on_core(place_ref[width // LANE], step)

        @pl.when(t == last)
        def _():
            for m in range(width // LANE):
                at = pl.multiple_of(place_ref[m] * LANE, LANE)
                o_ref[:, pl.ds(at, LANE)] = acc[:, m * LANE : (m + 1) * LANE].astype(BF16)

    return pl.pallas_call(
        kernel,
        grid_spec=pltpu.PrefetchScalarGridSpec(
            num_scalar_prefetch=1,
            grid=(blocks // pair,),
            in_specs=[pl.BlockSpec((pair, rows, cols), lambda t, place: (t, 0, 0))]
            + weight_specs(weights, pair),
            out_specs=pl.BlockSpec((rows, width), lambda t, place: (0, 0)),
            scratch_shapes=[pltpu.VMEM((rows, width), F32)],
        ),
        out_shape=jax.ShapeDtypeStruct((rows, width), BF16),
        compiler_params=params(32),
        cost_estimate=pl.CostEstimate(
            flops=2 * rows * width * blocks * cols,
            bytes_accessed=2 * width * blocks * cols,
            transcendentals=0,
        ),
        name="hidden_grads",
    )(place, grads, *weights)


def sum_over(x, axis):
    size = lax.axis_size(axis)
    reach = 1
    while reach < size:
        x = x + lax.ppermute(x, axis, [(i, i ^ reach) for i in range(size)])
        reach *= 2
    return x


def exchange(x):
    return lax.all_to_all(x, "tok", split_axis=0, concat_axis=0, tiled=True)


def body(student_hidden, teacher_values, value_weight, value_bias):
    seqs, toks, width = student_hidden.shape
    groups, parts = lax.axis_size("dp"), lax.axis_size("tok")
    cols = value_weight.shape[1]
    depth = width // groups

    piece = lax.dynamic_slice_in_dim(value_weight, lax.axis_index("dp") * depth, depth)
    piece = jnp.concatenate([piece, jnp.broadcast_to(value_bias, (8, cols))], axis=0)
    pieces = exchange(jnp.broadcast_to(piece, (parts, depth + 8, cols)))
    bias = pieces[:, depth : depth + 1]

    columns = split_columns(teacher_values.reshape(seqs * toks, -1), parts)
    teacher = exchange(columns)
    weights = gather_weight(pieces[:, :depth])
    probs = teacher_probs(teacher, seqs)

    place = blocks_of()
    rows = student_hidden.reshape(seqs * toks, width)
    values = project(rows, weights, bias, place)
    values = exchange(values)
    grads, total = head_grads(values, probs)
    grads = exchange(grads)
    hidden_grad = hidden_grads(grads, weights, place).reshape(student_hidden.shape)
    tokens = seqs * toks * parts * groups
    bias_grad = sum_over(total, "dp")[0] / math.sqrt(tokens)
    return (hidden_grad, bias_grad)


def solution(mesh):
    placed = (P("dp", "tok", None), P("dp", "tok", None), P(None, "tok"), P(None, "tok"))
    return jax.shard_map(
        body,
        mesh=mesh,
        in_specs=placed,
        out_specs=(P("dp", "tok", None), P("tok")),
        check_vma=False,
    )
```

```python
import math

import jax
import jax.numpy as jnp
from jax import lax
from jax.experimental import pallas as pl
from jax.experimental.pallas import tpu as pltpu
from jax.sharding import PartitionSpec as P


SH = 64
TH = 128
LOG2E = 1.4426950408889634
NT = (((1,), (1,)), ((), ()))
TN = (((0,), (0,)), ((), ()))
NN = (((1,), (0,)), ((), ()))
F32 = jnp.float32
BF16 = jnp.bfloat16


def dot(a, b, dims):
    return lax.dot_general(a, b, dims, preferred_element_type=F32)


def params(mib):
    return pltpu.CompilerParams(vmem_limit_bytes=mib << 20)


def split_columns(x, parts):
    rows, width = x.shape
    cols = width // parts

    def kernel(x_ref, o_ref):
        o_ref[0] = x_ref[...]

    return pl.pallas_call(
        kernel,
        grid=(parts,),
        in_specs=[pl.BlockSpec((rows, cols), lambda t: (0, t))],
        out_specs=pl.BlockSpec((1, rows, cols), lambda t: (t, 0, 0)),
        out_shape=jax.ShapeDtypeStruct((parts, rows, cols), x.dtype),
        name="split_columns",
    )(x)


def copies_of_piece(weight, bias, group, depth, copies):
    cols = weight.shape[1]

    def kernel(g_ref, b_ref, w_ref, o_ref, held, ready):
        at = pl.multiple_of(g_ref[0] * depth, depth)
        copy = pltpu.make_async_copy(w_ref.at[pl.ds(at, depth)], held, ready)
        copy.start()
        copy.wait()
        tail = jnp.broadcast_to(b_ref[...], (8, cols))
        for t in range(copies):
            o_ref[t, :depth] = held[...]
            o_ref[t, depth:] = tail

    return pl.pallas_call(
        kernel,
        in_specs=[
            pl.BlockSpec(memory_space=pltpu.SMEM),
            pl.BlockSpec(memory_space=pltpu.VMEM),
            pl.BlockSpec(memory_space=pltpu.HBM),
        ],
        out_specs=pl.BlockSpec(memory_space=pltpu.VMEM),
        out_shape=jax.ShapeDtypeStruct((copies, depth + 8, cols), BF16),
        scratch_shapes=[pltpu.VMEM((depth, cols), BF16), pltpu.SemaphoreType.DMA],
        name="copies_of_piece",
    )(group, bias, weight)


SIDE = 4
LANE = 128
TAKE = 8


def ring_pairs(shift, first):
    def place(x, y, c):
        return ((x % SIDE) * SIDE + y % SIDE) * 2 + c

    pairs = []
    for x in range(SIDE):
        for y in range(SIDE):
            for c in range(2):
                dx, dy = (shift, 0) if (c == 0) == first else (0, shift)
                pairs.append((place(x, y, c), place(x + dx, y + dy, c)))
    return pairs


def gather_weight(piece):
    def send(v, shift, first):
        return lax.ppermute(v, "dp", ring_pairs(shift, first))

    below, above, far = [send(piece, k, True) for k in (1, -1, 2)]
    own = [jnp.stack([piece, below]), jnp.stack([far, above])]
    down0, up1 = send(own[0], 1, False), send(own[1], -1, False)
    down1, up0 = send(own[1], 1, False), send(own[0], -1, False)
    far0, far1 = send(down0, 1, False), send(up1, -1, False)
    swap = [(d, d ^ 1) for d in range(2 * SIDE * SIDE)]
    mine, theirs = [], []
    for parts in (own, [down0, down1], [far0, far1], [up0, up1]):
        theirs += [lax.ppermute(v, "dp", swap) for v in parts]
        mine += parts
    return mine + theirs


def blocks_of():
    table = []
    for d in range(2 * SIDE * SIDE):
        x, y, c = d // (2 * SIDE), d // 2 % SIDE, d % 2
        table.append(
            [(x - j) % SIDE * SIDE + (y - b) % SIDE for j in range(SIDE) for b in range(SIDE)]
            + [c]
        )
    return lax.dynamic_index_in_dim(
        jnp.array(table, jnp.int32), lax.axis_index("dp"), keepdims=False
    )


def weight_block(held, t):
    half = SIDE // 2

    def pick(side, b, j):
        return held[side, 2 * b + j // half, j % half, t]

    rows = []
    for j in range(SIDE):
        for b in range(SIDE):
            rows += [pick(0, b, j), pick(1, j, b)]
    return jnp.concatenate(rows, axis=0)


class Stream:
    def __init__(self, refs, held, sems, core, take):
        self.refs, self.held, self.sems = refs, held, sems
        self.core, self.take = core, take

    def start(self):
        count = len(self.refs) // 2
        blocks = self.held.shape[3]
        for n in range(blocks // self.take):
            span = pl.ds(n * self.take, self.take)
            for a, ref in enumerate(self.refs):
                side = self.core if a < count else 1 - self.core
                pltpu.make_async_copy(
                    ref.at[:, span], self.held.at[side, a % count, :, span], self.sems.at[n]
                ).start()

    def wait(self, n):
        span = pl.ds(n * self.take, self.take)
        part = self.held.at[:, :, :, span]
        pltpu.make_async_copy(part, part, self.sems.at[n]).wait()


def project(hidden, weights, bias, place):
    rows, width = hidden.shape
    half, blocks, depth, cols = weights[0].shape
    pair = 2
    count = len(weights)
    chips = width // LANE

    def kernel(place_ref, h_ref, b_ref, *refs):
        w_refs, o_ref, raw, h, held, ready, sems = refs[:count], *refs[count:]
        copy = pltpu.make_async_copy(h_ref, raw, ready)
        copy.start()
        stream = Stream(w_refs, held, sems, place_ref[chips], TAKE)
        stream.start()
        copy.wait()
        for m in range(chips):
            at = pl.multiple_of(place_ref[m] * LANE, LANE)
            h[:, m * LANE : (m + 1) * LANE] = raw[:, pl.ds(at, LANE)]
        for n in range(blocks // pair):
            if n * pair % TAKE == 0:
                stream.wait(n * pair // TAKE)
            w = jnp.concatenate(
                [weight_block(held, n * pair + k) for k in range(pair)], axis=1
            )
            r = dot(h[...], w, NN)
            for k in range(pair):
                v = r[:, k * cols : (k + 1) * cols] + b_ref[n * pair + k].astype(F32)
                o_ref[n * pair + k] = v.astype(BF16)

    return pl.pallas_call(
        kernel,
        in_specs=[
            pl.BlockSpec(memory_space=pltpu.SMEM),
            pl.BlockSpec(memory_space=pltpu.HBM),
            pl.BlockSpec(memory_space=pltpu.VMEM),
        ]
        + [pl.BlockSpec(memory_space=pl.ANY)] * count,
        out_specs=pl.BlockSpec(memory_space=pltpu.VMEM),
        scratch_shapes=[
            pltpu.VMEM((rows, width), BF16),
            pltpu.VMEM((rows, width), BF16),
            pltpu.VMEM((2, count // 2, half, blocks, depth, cols), BF16),
            pltpu.SemaphoreType.DMA,
            pltpu.SemaphoreType.DMA((blocks // TAKE,)),
        ],
        out_shape=jax.ShapeDtypeStruct((blocks, rows, cols), BF16),
        compiler_params=params(32),
        cost_estimate=pl.CostEstimate(
            flops=2 * rows * width * blocks * cols,
            bytes_accessed=2 * width * blocks * cols,
            transcendentals=0,
        ),
        name="project",
    )(place, hidden, bias, *weights)


def soft(scores, scale, total):
    peak = jnp.max(scores, axis=1, keepdims=True)
    e = jnp.exp2((scores - peak) * scale)
    return e * (total / jnp.sum(e, axis=1, keepdims=True))


def teacher_probs(teacher, seqs):
    blocks, rows, width = teacher.shape
    toks = rows // seqs
    length = blocks * toks
    heads = width // TH
    step = 256
    t4 = teacher.reshape(blocks, seqs, toks, width)

    def kernel(t_ref, o_ref):
        i = pl.program_id(2)
        part = step // toks
        t = t_ref[...].reshape(length, TH)
        q = t_ref[pl.ds(i * part, part)].reshape(step, TH)
        o_ref[0, 0] = soft(dot(q, t, NT), LOG2E / math.sqrt(TH), float(length))

    return pl.pallas_call(
        kernel,
        grid=(seqs, heads, length // step),
        in_specs=[
            pl.BlockSpec((blocks, None, toks, TH), lambda s, h, i: (0, s, 0, h))
        ],
        out_specs=pl.BlockSpec((1, 1, step, length), lambda s, h, i: (s, h, i, 0)),
        out_shape=jax.ShapeDtypeStruct((seqs, heads, length, length), F32),
        compiler_params=params(40),
        cost_estimate=pl.CostEstimate(
            flops=2 * seqs * heads * length * length * TH,
            bytes_accessed=4 * seqs * heads * length * length,
            transcendentals=seqs * heads * length * length,
        ),
        name="teacher_probs",
    )(t4)


def head_grads(student, probs):
    seqs = probs.shape[0]
    blocks, both, cols = student.shape
    toks = both // seqs
    length = blocks * toks
    heads = cols // SH
    step = 512
    part = step // toks
    last = length // step - 1

    def kernel(s_ref, p_ref, o_ref, b_ref, rows, trans):
        i = pl.program_id(1)
        s = s_ref[...].reshape(length, cols)
        q = s_ref[pl.ds(i * part, part)].reshape(step, cols)
        lane = lax.broadcasted_iota(jnp.int32, (step, cols), 1) // SH
        here = jnp.zeros((step, cols), F32)
        across = jnp.zeros((cols, length), F32)
        for h in range(heads):
            qh = jnp.where(lane == h, q, jnp.zeros_like(q))
            p = soft(dot(qh, s, NT), LOG2E / math.sqrt(SH), float(length))
            g = (p - p_ref[0, h]).astype(BF16)
            here = jnp.where(lane == h, dot(g, s, NN), here)
            across = across + dot(qh, g, TN)
        rows[pl.ds(i * step, step)] = here

        @pl.when(i == 0)
        def _():
            trans[...] = across

        @pl.when(i > 0)
        def _():
            trans[...] += across

        @pl.when(i == last)
        def _():
            grad = ((rows[...] + trans[...].T) * (1.0 / math.sqrt(SH))).astype(BF16)
            o_ref[...] = grad.reshape(blocks, toks, cols)
            total = jnp.sum(grad.astype(F32), axis=0, keepdims=True)
            b_ref[...] = jnp.where(pl.program_id(0) == 0, total, b_ref[...] + total)

    grads, total = pl.pallas_call(
        kernel,
        grid=(seqs, length // step),
        in_specs=[
            pl.BlockSpec((blocks, None, toks, cols), lambda s, i: (0, s, 0, 0)),
            pl.BlockSpec((1, heads, step, length), lambda s, i: (s, 0, i, 0)),
        ],
        out_specs=[
            pl.BlockSpec((blocks, None, toks, cols), lambda s, i: (0, s, 0, 0)),
            pl.BlockSpec((1, cols), lambda s, i: (0, 0)),
        ],
        out_shape=[
            jax.ShapeDtypeStruct((blocks, seqs, toks, cols), BF16),
            jax.ShapeDtypeStruct((1, cols), F32),
        ],
        scratch_shapes=[pltpu.VMEM((length, cols), F32), pltpu.VMEM((cols, length), F32)],
        compiler_params=params(48),
        cost_estimate=pl.CostEstimate(
            flops=6 * seqs * heads * length * length * cols,
            bytes_accessed=4 * seqs * heads * length * length,
            transcendentals=seqs * heads * length * length,
        ),
        name="head_grads",
    )(student.reshape(blocks, seqs, toks, cols), probs)
    return grads.reshape(student.shape), total


def hidden_grads(grads, weights, place):
    blocks, rows, cols = grads.shape
    half, _, depth, _ = weights[0].shape
    count = len(weights)
    width = count * half * depth
    pair = 2
    chips = width // LANE

    def kernel(place_ref, g_ref, *refs):
        w_refs, o_ref, acc, held, sems = refs[:count], *refs[count:]
        stream = Stream(w_refs, held, sems, place_ref[chips], TAKE)
        stream.start()
        for n in range(blocks // pair):
            if n * pair % TAKE == 0:
                stream.wait(n * pair // TAKE)
            w = jnp.concatenate(
                [weight_block(held, n * pair + k) for k in range(pair)], axis=1
            )
            g = jnp.concatenate([g_ref[n * pair + k] for k in range(pair)], axis=1)
            r = dot(g, w, NT)
            if n == 0:
                acc[...] = r
            else:
                acc[...] += r
        for m in range(chips):
            at = pl.multiple_of(place_ref[m] * LANE, LANE)
            o_ref[:, pl.ds(at, LANE)] = acc[:, m * LANE : (m + 1) * LANE].astype(BF16)

    return pl.pallas_call(
        kernel,
        in_specs=[
            pl.BlockSpec(memory_space=pltpu.SMEM),
            pl.BlockSpec(memory_space=pltpu.VMEM),
        ]
        + [pl.BlockSpec(memory_space=pl.ANY)] * count,
        out_specs=pl.BlockSpec(memory_space=pltpu.VMEM),
        scratch_shapes=[
            pltpu.VMEM((rows, width), F32),
            pltpu.VMEM((2, count // 2, half, blocks, depth, cols), BF16),
            pltpu.SemaphoreType.DMA((blocks // TAKE,)),
        ],
        out_shape=jax.ShapeDtypeStruct((rows, width), BF16),
        compiler_params=params(32),
        cost_estimate=pl.CostEstimate(
            flops=2 * rows * width * blocks * cols,
            bytes_accessed=2 * width * blocks * cols,
            transcendentals=0,
        ),
        name="hidden_grads",
    )(place, grads, *weights)


def sum_over(x, axis):
    size = lax.axis_size(axis)
    reach = 1
    while reach < size:
        x = x + lax.ppermute(x, axis, [(i, i ^ reach) for i in range(size)])
        reach *= 2
    return x


def exchange(x):
    return lax.all_to_all(x, "tok", split_axis=0, concat_axis=0, tiled=True)


def body(student_hidden, teacher_values, value_weight, value_bias):
    seqs, toks, width = student_hidden.shape
    groups, parts = lax.axis_size("dp"), lax.axis_size("tok")
    depth = width // groups

    group = lax.axis_index("dp").astype(jnp.int32)[None]
    piece = copies_of_piece(value_weight, value_bias, group, depth, parts)
    pieces = exchange(piece)
    bias = pieces[:, depth : depth + 1]

    columns = split_columns(teacher_values.reshape(seqs * toks, -1), parts)
    teacher = exchange(columns)
    weights = gather_weight(pieces[:, :depth])
    probs = teacher_probs(teacher, seqs)

    place = blocks_of()
    rows = student_hidden.reshape(seqs * toks, width)
    values = project(rows, weights, bias, place)
    values = exchange(values)
    grads, total = head_grads(values, probs)
    grads = exchange(grads)
    hidden_grad = hidden_grads(grads, weights, place).reshape(student_hidden.shape)
    tokens = seqs * toks * parts * groups
    bias_grad = sum_over(total, "dp")[0] / math.sqrt(tokens)
    return (hidden_grad, bias_grad)


def solution(mesh):
    placed = (P("dp", "tok", None), P("dp", "tok", None), P(None, "tok"), P(None, "tok"))
    return jax.shard_map(
        body,
        mesh=mesh,
        in_specs=placed,
        out_specs=(P("dp", "tok", None), P("tok")),
        check_vma=False,
    )
```

```python
import math

import jax
import jax.numpy as jnp
from jax import lax
from jax.experimental import pallas as pl
from jax.experimental.pallas import tpu as pltpu
from jax.sharding import PartitionSpec as P


SH = 64
TH = 128
LOG2E = 1.4426950408889634
NT = (((1,), (1,)), ((), ()))
TN = (((0,), (0,)), ((), ()))
NN = (((1,), (0,)), ((), ()))
F32 = jnp.float32
BF16 = jnp.bfloat16


def dot(a, b, dims):
    return lax.dot_general(a, b, dims, preferred_element_type=F32)


def params(mib):
    return pltpu.CompilerParams(vmem_limit_bytes=mib << 20)


def split_columns(x, parts):
    rows, width = x.shape
    cols = width // parts

    def kernel(x_ref, o_ref):
        o_ref[0] = x_ref[...]

    return pl.pallas_call(
        kernel,
        grid=(parts,),
        in_specs=[pl.BlockSpec((rows, cols), lambda t: (0, t))],
        out_specs=pl.BlockSpec((1, rows, cols), lambda t: (t, 0, 0)),
        out_shape=jax.ShapeDtypeStruct((parts, rows, cols), x.dtype),
        name="split_columns",
    )(x)


def copies_of_piece(weight, bias, group, depth, copies):
    cols = weight.shape[1]

    def kernel(g_ref, b_ref, w_ref, o_ref, held, ready):
        at = pl.multiple_of(g_ref[0] * depth, depth)
        copy = pltpu.make_async_copy(w_ref.at[pl.ds(at, depth)], held, ready)
        copy.start()
        copy.wait()
        tail = jnp.broadcast_to(b_ref[...], (8, cols))
        for t in range(copies):
            o_ref[t, :depth] = held[...]
            o_ref[t, depth:] = tail

    return pl.pallas_call(
        kernel,
        in_specs=[
            pl.BlockSpec(memory_space=pltpu.SMEM),
            pl.BlockSpec(memory_space=pltpu.VMEM),
            pl.BlockSpec(memory_space=pltpu.HBM),
        ],
        out_specs=pl.BlockSpec(memory_space=pltpu.VMEM),
        out_shape=jax.ShapeDtypeStruct((copies, depth + 8, cols), BF16),
        scratch_shapes=[pltpu.VMEM((depth, cols), BF16), pltpu.SemaphoreType.DMA],
        name="copies_of_piece",
    )(group, bias, weight)


SIDE = 4
LANE = 128
TAKE = 8


def ring_pairs(shift, first):
    def place(x, y, c):
        return ((x % SIDE) * SIDE + y % SIDE) * 2 + c

    pairs = []
    for x in range(SIDE):
        for y in range(SIDE):
            for c in range(2):
                dx, dy = (shift, 0) if (c == 0) == first else (0, shift)
                pairs.append((place(x, y, c), place(x + dx, y + dy, c)))
    return pairs


def gather_weight(piece):
    def send(v, shift, first):
        return lax.ppermute(v, "dp", ring_pairs(shift, first))

    below, above, far = [send(piece, k, True) for k in (1, -1, 2)]
    own = [jnp.stack([piece, below]), jnp.stack([far, above])]
    down0, up1 = send(own[0], 1, False), send(own[1], -1, False)
    down1, up0 = send(own[1], 1, False), send(own[0], -1, False)
    far0, far1 = send(down0, 1, False), send(up1, -1, False)
    return own + [down0, down1, far0, far1, up0, up1]


def swap_cores(values):
    swap = [(d, d ^ 1) for d in range(2 * SIDE * SIDE)]
    return [lax.ppermute(v, "dp", swap) for v in values]


def blocks_of():
    table = []
    for d in range(2 * SIDE * SIDE):
        x, y, c = d // (2 * SIDE), d // 2 % SIDE, d % 2
        table.append(
            [(x - j) % SIDE * SIDE + (y - b) % SIDE for j in range(SIDE) for b in range(SIDE)]
            + [c]
        )
    return lax.dynamic_index_in_dim(
        jnp.array(table, jnp.int32), lax.axis_index("dp"), keepdims=False
    )


def weight_block(held, t):
    half = SIDE // 2

    def pick(side, b, j):
        return held[side, 2 * b + j // half, j % half, t]

    rows = []
    for j in range(SIDE):
        for b in range(SIDE):
            rows += [pick(0, b, j), pick(1, j, b)]
    return jnp.concatenate(rows, axis=0)


class Stream:
    def __init__(self, refs, held, sems, core, take):
        self.refs, self.held, self.sems = refs, held, sems
        self.core, self.take = core, take

    def start(self):
        sides, count, _, blocks = self.held.shape[:4]
        for n in range(blocks // self.take):
            span = pl.ds(n * self.take, self.take)
            for a, ref in enumerate(self.refs):
                side = 0 if sides == 1 else self.core if a < count else 1 - self.core
                pltpu.make_async_copy(
                    ref.at[:, span], self.held.at[side, a % count, :, span], self.sems.at[n]
                ).start()

    def wait(self, n):
        span = pl.ds(n * self.take, self.take)
        part = self.held.at[:, :, :, span]
        pltpu.make_async_copy(part, part, self.sems.at[n]).wait()


def project(mine, theirs, weights, place):
    rows, width = mine.shape
    half, blocks, depth, cols = weights[0].shape
    pair = 2
    count = len(weights)
    chips = width // LANE

    def kernel(place_ref, m_ref, t_ref, *refs):
        w_refs, a_ref, z_ref, raw, h, held, ready, sems = refs[:count], *refs[count:]
        copies = [
            pltpu.make_async_copy(ref, raw.at[pl.ds(n * rows, rows)], ready.at[n])
            for n, ref in enumerate((m_ref, t_ref))
        ]
        for copy in copies:
            copy.start()
        core = place_ref[chips]
        stream = Stream(w_refs, held, sems, core, TAKE)
        stream.start()
        for copy in copies:
            copy.wait()

        def line_up(c):
            parts = []
            for b in range(SIDE):
                for j in range(SIDE):
                    m = j * SIDE + b if c == 0 else b * SIDE + j
                    at = pl.multiple_of(place_ref[m] * LANE, LANE)
                    parts.append(raw[:, pl.ds(at, LANE)][:, c * depth : (c + 1) * depth])
            for n in range(0, chips, 2):
                h[:, n * depth : (n + 2) * depth] = jnp.concatenate(parts[n : n + 2], axis=1)

        for c in range(2):
            pl.when(core == c)(lambda c=c: line_up(c))
        for n in range(blocks // pair):
            if n * pair % TAKE == 0:
                stream.wait(n * pair // TAKE)
            w = jnp.concatenate(
                [
                    jnp.concatenate(
                        [held[0, a, i, n * pair + k] for a in range(count) for i in range(half)],
                        axis=0,
                    )
                    for k in range(pair)
                ],
                axis=1,
            )
            r = dot(h[...], w, NN)
            for k in range(pair):
                v = r[:, k * cols : (k + 1) * cols]
                a_ref[n * pair + k] = v[:rows]
                z_ref[n * pair + k] = v[rows:]

    return pl.pallas_call(
        kernel,
        in_specs=[pl.BlockSpec(memory_space=pltpu.SMEM)]
        + [pl.BlockSpec(memory_space=pl.ANY)] * (2 + count),
        out_specs=[pl.BlockSpec(memory_space=pltpu.VMEM)] * 2,
        scratch_shapes=[
            pltpu.VMEM((2 * rows, width), BF16),
            pltpu.VMEM((2 * rows, width // 2), BF16),
            pltpu.VMEM((1, count, half, blocks, depth, cols), BF16),
            pltpu.SemaphoreType.DMA((2,)),
            pltpu.SemaphoreType.DMA((blocks // TAKE,)),
        ],
        out_shape=[jax.ShapeDtypeStruct((blocks, rows, cols), F32)] * 2,
        compiler_params=params(32),
        cost_estimate=pl.CostEstimate(
            flops=2 * rows * width * blocks * cols,
            bytes_accessed=width * blocks * cols,
            transcendentals=0,
        ),
        name="project",
    )(place, mine, theirs, *weights)


def soft(scores, scale, total):
    peak = jnp.max(scores, axis=1, keepdims=True)
    e = jnp.exp2((scores - peak) * scale)
    return e * (total / jnp.sum(e, axis=1, keepdims=True))


def teacher_probs(teacher, seqs):
    blocks, rows, width = teacher.shape
    toks = rows // seqs
    length = blocks * toks
    heads = width // TH
    step = 256
    t4 = teacher.reshape(blocks, seqs, toks, width)

    def kernel(t_ref, o_ref):
        i = pl.program_id(2)
        part = step // toks
        t = t_ref[...].reshape(length, TH)
        q = t_ref[pl.ds(i * part, part)].reshape(step, TH)
        o_ref[0, 0] = soft(dot(q, t, NT), LOG2E / math.sqrt(TH), float(length))

    return pl.pallas_call(
        kernel,
        grid=(seqs, heads, length // step),
        in_specs=[
            pl.BlockSpec((blocks, None, toks, TH), lambda s, h, i: (0, s, 0, h))
        ],
        out_specs=pl.BlockSpec((1, 1, step, length), lambda s, h, i: (s, h, i, 0)),
        out_shape=jax.ShapeDtypeStruct((seqs, heads, length, length), F32),
        compiler_params=params(40),
        cost_estimate=pl.CostEstimate(
            flops=2 * seqs * heads * length * length * TH,
            bytes_accessed=4 * seqs * heads * length * length,
            transcendentals=seqs * heads * length * length,
        ),
        name="teacher_probs",
    )(t4)


def head_grads(student, probs):
    seqs = probs.shape[0]
    blocks, both, cols = student.shape
    toks = both // seqs
    length = blocks * toks
    heads = cols // SH
    step = 512
    part = step // toks
    last = length // step - 1

    def kernel(s_ref, p_ref, o_ref, b_ref, rows, trans):
        i = pl.program_id(1)
        s = s_ref[...].reshape(length, cols)
        q = s_ref[pl.ds(i * part, part)].reshape(step, cols)
        lane = lax.broadcasted_iota(jnp.int32, (step, cols), 1) // SH
        here = jnp.zeros((step, cols), F32)
        across = jnp.zeros((cols, length), F32)
        for h in range(heads):
            qh = jnp.where(lane == h, q, jnp.zeros_like(q))
            p = soft(dot(qh, s, NT), LOG2E / math.sqrt(SH), float(length))
            g = (p - p_ref[0, h]).astype(BF16)
            here = jnp.where(lane == h, dot(g, s, NN), here)
            across = across + dot(qh, g, TN)
        rows[pl.ds(i * step, step)] = here

        @pl.when(i == 0)
        def _():
            trans[...] = across

        @pl.when(i > 0)
        def _():
            trans[...] += across

        @pl.when(i == last)
        def _():
            grad = ((rows[...] + trans[...].T) * (1.0 / math.sqrt(SH))).astype(BF16)
            o_ref[...] = grad.reshape(blocks, toks, cols)
            total = jnp.sum(grad.astype(F32), axis=0, keepdims=True)
            b_ref[...] = jnp.where(pl.program_id(0) == 0, total, b_ref[...] + total)

    grads, total = pl.pallas_call(
        kernel,
        grid=(seqs, length // step),
        in_specs=[
            pl.BlockSpec((blocks, None, toks, cols), lambda s, i: (0, s, 0, 0)),
            pl.BlockSpec((1, heads, step, length), lambda s, i: (s, 0, i, 0)),
        ],
        out_specs=[
            pl.BlockSpec((blocks, None, toks, cols), lambda s, i: (0, s, 0, 0)),
            pl.BlockSpec((1, cols), lambda s, i: (0, 0)),
        ],
        out_shape=[
            jax.ShapeDtypeStruct((blocks, seqs, toks, cols), BF16),
            jax.ShapeDtypeStruct((1, cols), F32),
        ],
        scratch_shapes=[pltpu.VMEM((length, cols), F32), pltpu.VMEM((cols, length), F32)],
        compiler_params=params(48),
        cost_estimate=pl.CostEstimate(
            flops=6 * seqs * heads * length * length * cols,
            bytes_accessed=4 * seqs * heads * length * length,
            transcendentals=seqs * heads * length * length,
        ),
        name="head_grads",
    )(student.reshape(blocks, seqs, toks, cols), probs)
    return grads.reshape(student.shape), total


def hidden_grads(grads, weights, place):
    blocks, rows, cols = grads.shape
    half, _, depth, _ = weights[0].shape
    count = len(weights)
    width = count * half * depth
    pair = 2
    chips = width // LANE

    def kernel(place_ref, g_ref, *refs):
        w_refs, o_ref, acc, held, sems = refs[:count], *refs[count:]
        stream = Stream(w_refs, held, sems, place_ref[chips], TAKE)
        stream.start()
        for n in range(blocks // pair):
            if n * pair % TAKE == 0:
                stream.wait(n * pair // TAKE)
            w = jnp.concatenate(
                [weight_block(held, n * pair + k) for k in range(pair)], axis=1
            )
            g = jnp.concatenate([g_ref[n * pair + k] for k in range(pair)], axis=1)
            r = dot(g, w, NT)
            if n == 0:
                acc[...] = r
            else:
                acc[...] += r
        for m in range(chips):
            at = pl.multiple_of(place_ref[m] * LANE, LANE)
            o_ref[:, pl.ds(at, LANE)] = acc[:, m * LANE : (m + 1) * LANE].astype(BF16)

    return pl.pallas_call(
        kernel,
        in_specs=[
            pl.BlockSpec(memory_space=pltpu.SMEM),
            pl.BlockSpec(memory_space=pltpu.VMEM),
        ]
        + [pl.BlockSpec(memory_space=pl.ANY)] * count,
        out_specs=pl.BlockSpec(memory_space=pltpu.VMEM),
        scratch_shapes=[
            pltpu.VMEM((rows, width), F32),
            pltpu.VMEM((2, count // 2, half, blocks, depth, cols), BF16),
            pltpu.SemaphoreType.DMA((blocks // TAKE,)),
        ],
        out_shape=jax.ShapeDtypeStruct((rows, width), BF16),
        compiler_params=params(32),
        cost_estimate=pl.CostEstimate(
            flops=2 * rows * width * blocks * cols,
            bytes_accessed=2 * width * blocks * cols,
            transcendentals=0,
        ),
        name="hidden_grads",
    )(place, grads, *weights)


def sum_over(x, axis):
    size = lax.axis_size(axis)
    reach = 1
    while reach < size:
        x = x + lax.ppermute(x, axis, [(i, i ^ reach) for i in range(size)])
        reach *= 2
    return x


def exchange(x):
    return lax.all_to_all(x, "tok", split_axis=0, concat_axis=0, tiled=True)


def body(student_hidden, teacher_values, value_weight, value_bias):
    seqs, toks, width = student_hidden.shape
    groups, parts = lax.axis_size("dp"), lax.axis_size("tok")
    depth = width // groups

    group = lax.axis_index("dp").astype(jnp.int32)[None]
    piece = copies_of_piece(value_weight, value_bias, group, depth, parts)
    pieces = exchange(piece)
    bias = pieces[:, depth : depth + 1]

    columns = split_columns(teacher_values.reshape(seqs * toks, -1), parts)
    teacher = exchange(columns)
    weights = gather_weight(pieces[:, :depth])
    probs = teacher_probs(teacher, seqs)

    place = blocks_of()
    rows = student_hidden.reshape(seqs * toks, width)
    other_rows = swap_cores([rows])[0]
    kept, sent = project(rows, other_rows, weights, place)
    got = swap_cores([sent])[0]
    values = (kept + got + bias.astype(F32)).astype(BF16)
    values = exchange(values)
    weights = weights + swap_cores(weights)
    grads, total = head_grads(values, probs)
    grads = exchange(grads)
    hidden_grad = hidden_grads(grads, weights, place).reshape(student_hidden.shape)
    tokens = seqs * toks * parts * groups
    bias_grad = sum_over(total, "dp")[0] / math.sqrt(tokens)
    return (hidden_grad, bias_grad)


def solution(mesh):
    placed = (P("dp", "tok", None), P("dp", "tok", None), P(None, "tok"), P(None, "tok"))
    return jax.shard_map(
        body,
        mesh=mesh,
        in_specs=placed,
        out_specs=(P("dp", "tok", None), P("tok")),
        check_vma=False,
    )
```

```python
import math

import jax
import jax.numpy as jnp
from jax import lax
from jax.experimental import pallas as pl
from jax.experimental.pallas import tpu as pltpu
from jax.sharding import PartitionSpec as P


SH = 64
TH = 128
LOG2E = 1.4426950408889634
NT = (((1,), (1,)), ((), ()))
TN = (((0,), (0,)), ((), ()))
NN = (((1,), (0,)), ((), ()))
F32 = jnp.float32
BF16 = jnp.bfloat16


def dot(a, b, dims):
    return lax.dot_general(a, b, dims, preferred_element_type=F32)


def params(mib):
    return pltpu.CompilerParams(vmem_limit_bytes=mib << 20)


def split_columns(x, parts):
    rows, width = x.shape
    cols = width // parts

    def kernel(x_ref, o_ref):
        o_ref[0] = x_ref[...]

    return pl.pallas_call(
        kernel,
        grid=(parts,),
        in_specs=[pl.BlockSpec((rows, cols), lambda t: (0, t))],
        out_specs=pl.BlockSpec((1, rows, cols), lambda t: (t, 0, 0)),
        out_shape=jax.ShapeDtypeStruct((parts, rows, cols), x.dtype),
        name="split_columns",
    )(x)


def copies_of_piece(weight, bias, group, depth, copies):
    cols = weight.shape[1]

    def kernel(g_ref, b_ref, w_ref, o_ref, held, ready):
        at = pl.multiple_of(g_ref[0] * depth, depth)
        copy = pltpu.make_async_copy(w_ref.at[pl.ds(at, depth)], held, ready)
        copy.start()
        copy.wait()
        tail = jnp.broadcast_to(b_ref[...], (8, cols))
        for t in range(copies):
            o_ref[t, :depth] = held[...]
            o_ref[t, depth:] = tail

    return pl.pallas_call(
        kernel,
        in_specs=[
            pl.BlockSpec(memory_space=pltpu.SMEM),
            pl.BlockSpec(memory_space=pltpu.VMEM),
            pl.BlockSpec(memory_space=pltpu.HBM),
        ],
        out_specs=pl.BlockSpec(memory_space=pltpu.VMEM),
        out_shape=jax.ShapeDtypeStruct((copies, depth + 8, cols), BF16),
        scratch_shapes=[pltpu.VMEM((depth, cols), BF16), pltpu.SemaphoreType.DMA],
        name="copies_of_piece",
    )(group, bias, weight)


SIDE = 4
LANE = 128
TAKE = 8
EARLY = 3


def ring_pairs(shift, first):
    def place(x, y, c):
        return ((x % SIDE) * SIDE + y % SIDE) * 2 + c

    pairs = []
    for x in range(SIDE):
        for y in range(SIDE):
            for c in range(2):
                dx, dy = (shift, 0) if (c == 0) == first else (0, shift)
                pairs.append((place(x, y, c), place(x + dx, y + dy, c)))
    return pairs


def gather_weight(piece):
    def send(v, shift, first):
        return lax.ppermute(v, "dp", ring_pairs(shift, first))

    below, above, far = [send(piece, k, True) for k in (1, -1, 2)]
    own = [jnp.stack([piece, below]), jnp.stack([far, above])]
    down0, up1 = send(own[0], 1, False), send(own[1], -1, False)
    down1, up0 = send(own[1], 1, False), send(own[0], -1, False)
    far0, far1 = send(down0, 1, False), send(up1, -1, False)
    return own + [down0, down1, far0, far1, up0, up1]


def swap_cores(values):
    swap = [(d, d ^ 1) for d in range(2 * SIDE * SIDE)]
    return [lax.ppermute(v, "dp", swap) for v in values]


def blocks_of():
    table = []
    for d in range(2 * SIDE * SIDE):
        x, y, c = d // (2 * SIDE), d // 2 % SIDE, d % 2
        table.append(
            [(x - j) % SIDE * SIDE + (y - b) % SIDE for j in range(SIDE) for b in range(SIDE)]
            + [c]
        )
    return lax.dynamic_index_in_dim(
        jnp.array(table, jnp.int32), lax.axis_index("dp"), keepdims=False
    )


def weight_block(held, t):
    half = SIDE // 2

    def pick(side, b, j):
        return held[side, 2 * b + j // half, j % half, t]

    rows = []
    for j in range(SIDE):
        for b in range(SIDE):
            rows += [pick(0, b, j), pick(1, j, b)]
    return jnp.concatenate(rows, axis=0)


class Stream:
    def __init__(self, refs, held, sems, core, take):
        self.refs, self.held, self.sems = refs, held, sems
        self.core, self.take = core, take

    def start(self):
        sides, count, _, blocks = self.held.shape[:4]
        for n in range(blocks // self.take):
            span = pl.ds(n * self.take, self.take)
            for a, ref in enumerate(self.refs):
                side = 0 if sides == 1 else self.core if a < count else 1 - self.core
                pltpu.make_async_copy(
                    ref.at[:, span], self.held.at[side, a % count, :, span], self.sems.at[n]
                ).start()

    def wait(self, n):
        span = pl.ds(n * self.take, self.take)
        part = self.held.at[:, :, :, span]
        pltpu.make_async_copy(part, part, self.sems.at[n]).wait()


def project(mine, theirs, weights, place):
    rows, width = mine.shape
    half, blocks, depth, cols = weights[0].shape
    pair = 2
    count = len(weights)
    chips = width // LANE

    def kernel(place_ref, m_ref, t_ref, *refs):
        w_refs, a_ref, z_ref, raw, h, held, ready, sems = refs[:count], *refs[count:]
        copies = [
            pltpu.make_async_copy(ref, raw.at[pl.ds(n * rows, rows)], ready.at[n])
            for n, ref in enumerate((m_ref, t_ref))
        ]
        for copy in copies:
            copy.start()
        core = place_ref[chips]
        stream = Stream(w_refs, held, sems, core, TAKE)
        stream.start()
        for copy in copies:
            copy.wait()

        def line_up(c):
            parts = []
            for b in range(SIDE):
                for j in range(SIDE):
                    m = j * SIDE + b if c == 0 else b * SIDE + j
                    at = pl.multiple_of(place_ref[m] * LANE, LANE)
                    parts.append(raw[:, pl.ds(at, LANE)][:, c * depth : (c + 1) * depth])
            for n in range(0, chips, 2):
                h[:, n * depth : (n + 2) * depth] = jnp.concatenate(parts[n : n + 2], axis=1)

        for c in range(2):
            pl.when(core == c)(lambda c=c: line_up(c))
        for n in range(blocks // pair):
            if n * pair % TAKE == 0:
                stream.wait(n * pair // TAKE)
            w = jnp.concatenate(
                [
                    jnp.concatenate(
                        [held[0, a, i, n * pair + k] for a in range(count) for i in range(half)],
                        axis=0,
                    )
                    for k in range(pair)
                ],
                axis=1,
            )
            r = dot(h[...], w, NN)
            for k in range(pair):
                v = r[:, k * cols : (k + 1) * cols]
                a_ref[n * pair + k] = v[:rows]
                z_ref[n * pair + k] = v[rows:]

    return pl.pallas_call(
        kernel,
        in_specs=[pl.BlockSpec(memory_space=pltpu.SMEM)]
        + [pl.BlockSpec(memory_space=pl.ANY)] * (2 + count),
        out_specs=[pl.BlockSpec(memory_space=pltpu.VMEM)] * 2,
        scratch_shapes=[
            pltpu.VMEM((2 * rows, width), BF16),
            pltpu.VMEM((2 * rows, width // 2), BF16),
            pltpu.VMEM((1, count, half, blocks, depth, cols), BF16),
            pltpu.SemaphoreType.DMA((2,)),
            pltpu.SemaphoreType.DMA((blocks // TAKE,)),
        ],
        out_shape=[jax.ShapeDtypeStruct((blocks, rows, cols), F32)] * 2,
        compiler_params=params(32),
        cost_estimate=pl.CostEstimate(
            flops=2 * rows * width * blocks * cols,
            bytes_accessed=width * blocks * cols,
            transcendentals=0,
        ),
        name="project",
    )(place, mine, theirs, *weights)


def soft(scores, scale, total):
    peak = jnp.max(scores, axis=1, keepdims=True)
    e = jnp.exp2((scores - peak) * scale)
    return e * (total / jnp.sum(e, axis=1, keepdims=True))


def teacher_probs(teacher, seqs):
    blocks, rows, width = teacher.shape
    toks = rows // seqs
    length = blocks * toks
    heads = width // TH
    step = 256
    t4 = teacher.reshape(blocks, seqs, toks, width)

    def kernel(t_ref, o_ref):
        i = pl.program_id(2)
        part = step // toks
        t = t_ref[...].reshape(length, TH)
        q = t_ref[pl.ds(i * part, part)].reshape(step, TH)
        o_ref[0, 0] = soft(dot(q, t, NT), LOG2E / math.sqrt(TH), float(length))

    return pl.pallas_call(
        kernel,
        grid=(seqs, heads, length // step),
        in_specs=[
            pl.BlockSpec((blocks, None, toks, TH), lambda s, h, i: (0, s, 0, h))
        ],
        out_specs=pl.BlockSpec((1, 1, step, length), lambda s, h, i: (s, h, i, 0)),
        out_shape=jax.ShapeDtypeStruct((seqs, heads, length, length), F32),
        compiler_params=params(40),
        cost_estimate=pl.CostEstimate(
            flops=2 * seqs * heads * length * length * TH,
            bytes_accessed=4 * seqs * heads * length * length,
            transcendentals=seqs * heads * length * length,
        ),
        name="teacher_probs",
    )(t4)


def head_grads(student, probs):
    seqs = probs.shape[0]
    blocks, both, cols = student.shape
    toks = both // seqs
    length = blocks * toks
    heads = cols // SH
    step = 512
    part = step // toks
    last = length // step - 1

    def kernel(s_ref, p_ref, o_ref, b_ref, rows, trans):
        i = pl.program_id(1)
        s = s_ref[...].reshape(length, cols)
        q = s_ref[pl.ds(i * part, part)].reshape(step, cols)
        lane = lax.broadcasted_iota(jnp.int32, (step, cols), 1) // SH
        here = jnp.zeros((step, cols), F32)
        across = jnp.zeros((cols, length), F32)
        for h in range(heads):
            qh = jnp.where(lane == h, q, jnp.zeros_like(q))
            p = soft(dot(qh, s, NT), LOG2E / math.sqrt(SH), float(length))
            g = (p - p_ref[0, h]).astype(BF16)
            here = jnp.where(lane == h, dot(g, s, NN), here)
            across = across + dot(qh, g, TN)
        rows[pl.ds(i * step, step)] = here

        @pl.when(i == 0)
        def _():
            trans[...] = across

        @pl.when(i > 0)
        def _():
            trans[...] += across

        @pl.when(i == last)
        def _():
            grad = ((rows[...] + trans[...].T) * (1.0 / math.sqrt(SH))).astype(BF16)
            o_ref[...] = grad.reshape(blocks, toks, cols)
            total = jnp.sum(grad.astype(F32), axis=0, keepdims=True)
            b_ref[...] = jnp.where(pl.program_id(0) == 0, total, b_ref[...] + total)

    grads, total = pl.pallas_call(
        kernel,
        grid=(seqs, length // step),
        in_specs=[
            pl.BlockSpec((blocks, None, toks, cols), lambda s, i: (0, s, 0, 0)),
            pl.BlockSpec((1, heads, step, length), lambda s, i: (s, 0, i, 0)),
        ],
        out_specs=[
            pl.BlockSpec((blocks, None, toks, cols), lambda s, i: (0, s, 0, 0)),
            pl.BlockSpec((1, cols), lambda s, i: (0, 0)),
        ],
        out_shape=[
            jax.ShapeDtypeStruct((blocks, seqs, toks, cols), BF16),
            jax.ShapeDtypeStruct((1, cols), F32),
        ],
        scratch_shapes=[pltpu.VMEM((length, cols), F32), pltpu.VMEM((cols, length), F32)],
        compiler_params=params(58),
        cost_estimate=pl.CostEstimate(
            flops=6 * seqs * heads * length * length * cols,
            bytes_accessed=4 * seqs * heads * length * length,
            transcendentals=seqs * heads * length * length,
        ),
        name="head_grads",
    )(student.reshape(blocks, seqs, toks, cols), probs)
    return grads.reshape(student.shape), total


def hidden_grads(grads, weights, place):
    blocks, rows, cols = grads.shape
    half, _, depth, _ = weights[0].shape
    count = len(weights)
    width = count * half * depth
    pair = 2
    chips = width // LANE

    def kernel(place_ref, g_ref, *refs):
        w_refs, o_ref, acc, held, sems = refs[:count], *refs[count:]
        stream = Stream(w_refs, held, sems, place_ref[chips], TAKE)
        stream.start()
        for n in range(blocks // pair):
            if n * pair % TAKE == 0:
                stream.wait(n * pair // TAKE)
            w = jnp.concatenate(
                [weight_block(held, n * pair + k) for k in range(pair)], axis=1
            )
            g = jnp.concatenate([g_ref[n * pair + k] for k in range(pair)], axis=1)
            r = dot(g, w, NT)
            if n == 0:
                acc[...] = r
            else:
                acc[...] += r
        for m in range(chips):
            at = pl.multiple_of(place_ref[m] * LANE, LANE)
            o_ref[:, pl.ds(at, LANE)] = acc[:, m * LANE : (m + 1) * LANE].astype(BF16)

    return pl.pallas_call(
        kernel,
        in_specs=[
            pl.BlockSpec(memory_space=pltpu.SMEM),
            pl.BlockSpec(memory_space=pltpu.VMEM),
        ]
        + [pl.BlockSpec(memory_space=pl.ANY)] * count,
        out_specs=pl.BlockSpec(memory_space=pltpu.VMEM),
        scratch_shapes=[
            pltpu.VMEM((rows, width), F32),
            pltpu.VMEM((2, count // 2, half, blocks, depth, cols), BF16),
            pltpu.SemaphoreType.DMA((blocks // TAKE,)),
        ],
        out_shape=jax.ShapeDtypeStruct((rows, width), BF16),
        compiler_params=params(32),
        cost_estimate=pl.CostEstimate(
            flops=2 * rows * width * blocks * cols,
            bytes_accessed=2 * width * blocks * cols,
            transcendentals=0,
        ),
        name="hidden_grads",
    )(place, grads, *weights)


def sum_over(x, axis):
    size = lax.axis_size(axis)
    reach = 1
    while reach < size:
        x = x + lax.ppermute(x, axis, [(i, i ^ reach) for i in range(size)])
        reach *= 2
    return x


def exchange(x):
    return lax.all_to_all(x, "tok", split_axis=0, concat_axis=0, tiled=True)


def body(student_hidden, teacher_values, value_weight, value_bias):
    seqs, toks, width = student_hidden.shape
    groups, parts = lax.axis_size("dp"), lax.axis_size("tok")
    depth = width // groups

    group = lax.axis_index("dp").astype(jnp.int32)[None]
    piece = copies_of_piece(value_weight, value_bias, group, depth, parts)
    pieces = exchange(piece)
    bias = pieces[:, depth : depth + 1]

    columns = split_columns(teacher_values.reshape(seqs * toks, -1), parts)
    teacher = exchange(columns)
    weights = gather_weight(pieces[:, :depth])
    probs = teacher_probs(teacher, seqs)

    place = blocks_of()
    rows = student_hidden.reshape(seqs * toks, width)
    other_rows = swap_cores([rows])[0]
    swapped = swap_cores(weights[:EARLY])
    kept, sent = project(rows, other_rows, weights, place)
    got = swap_cores([sent])[0]
    values = (kept + got + bias.astype(F32)).astype(BF16)
    values = exchange(values)
    weights = weights + swapped + swap_cores(weights[EARLY:])
    grads, total = head_grads(values, probs)
    grads = exchange(grads)
    hidden_grad = hidden_grads(grads, weights, place).reshape(student_hidden.shape)
    tokens = seqs * toks * parts * groups
    bias_grad = sum_over(total, "dp")[0] / math.sqrt(tokens)
    return (hidden_grad, bias_grad)


def solution(mesh):
    placed = (P("dp", "tok", None), P("dp", "tok", None), P(None, "tok"), P(None, "tok"))
    return jax.shard_map(
        body,
        mesh=mesh,
        in_specs=placed,
        out_specs=(P("dp", "tok", None), P("tok")),
        check_vma=False,
    )
```

```python
import math

import jax
import jax.numpy as jnp
from jax import lax
from jax.experimental import pallas as pl
from jax.experimental.pallas import tpu as pltpu
from jax.sharding import PartitionSpec as P


SH = 64
TH = 128
LOG2E = 1.4426950408889634
NT = (((1,), (1,)), ((), ()))
TN = (((0,), (0,)), ((), ()))
NN = (((1,), (0,)), ((), ()))
F32 = jnp.float32
BF16 = jnp.bfloat16


def dot(a, b, dims):
    return lax.dot_general(a, b, dims, preferred_element_type=F32)


def params(mib):
    return pltpu.CompilerParams(vmem_limit_bytes=mib << 20)


def split_columns(x, parts):
    rows, width = x.shape
    cols = width // parts

    def kernel(x_ref, o_ref):
        o_ref[0] = x_ref[...]

    return pl.pallas_call(
        kernel,
        grid=(parts,),
        in_specs=[pl.BlockSpec((rows, cols), lambda t: (0, t))],
        out_specs=pl.BlockSpec((1, rows, cols), lambda t: (t, 0, 0)),
        out_shape=jax.ShapeDtypeStruct((parts, rows, cols), x.dtype),
        name="split_columns",
    )(x)


def copies_of_piece(weight, bias, group, depth, copies):
    cols = weight.shape[1]

    def kernel(g_ref, b_ref, w_ref, o_ref, held, ready):
        at = pl.multiple_of(g_ref[0] * depth, depth)
        copy = pltpu.make_async_copy(w_ref.at[pl.ds(at, depth)], held, ready)
        copy.start()
        copy.wait()
        tail = jnp.broadcast_to(b_ref[...], (8, cols))
        for t in range(copies):
            o_ref[t, :depth] = held[...]
            o_ref[t, depth:] = tail

    return pl.pallas_call(
        kernel,
        in_specs=[
            pl.BlockSpec(memory_space=pltpu.SMEM),
            pl.BlockSpec(memory_space=pltpu.VMEM),
            pl.BlockSpec(memory_space=pltpu.HBM),
        ],
        out_specs=pl.BlockSpec(memory_space=pltpu.VMEM),
        out_shape=jax.ShapeDtypeStruct((copies, depth + 8, cols), BF16),
        scratch_shapes=[pltpu.VMEM((depth, cols), BF16), pltpu.SemaphoreType.DMA],
        name="copies_of_piece",
    )(group, bias, weight)


SIDE = 4
LANE = 128
TAKE = 8
EARLY = 4


def ring_pairs(shift, first):
    def place(x, y, c):
        return ((x % SIDE) * SIDE + y % SIDE) * 2 + c

    pairs = []
    for x in range(SIDE):
        for y in range(SIDE):
            for c in range(2):
                dx, dy = (shift, 0) if (c == 0) == first else (0, shift)
                pairs.append((place(x, y, c), place(x + dx, y + dy, c)))
    return pairs


def gather_weight(piece):
    def send(v, shift, first):
        return lax.ppermute(v, "dp", ring_pairs(shift, first))

    below, above, far = [send(piece, k, True) for k in (1, -1, 2)]
    own = [jnp.stack([piece, below]), jnp.stack([far, above])]
    down0, up1 = send(own[0], 1, False), send(own[1], -1, False)
    down1, up0 = send(own[1], 1, False), send(own[0], -1, False)
    far0, far1 = send(down0, 1, False), send(up1, -1, False)
    return own + [down0, down1, far0, far1, up0, up1]


def swap_cores(values):
    swap = [(d, d ^ 1) for d in range(2 * SIDE * SIDE)]
    return [lax.ppermute(v, "dp", swap) for v in values]


def blocks_of():
    table = []
    for d in range(2 * SIDE * SIDE):
        x, y, c = d // (2 * SIDE), d // 2 % SIDE, d % 2
        table.append(
            [(x - j) % SIDE * SIDE + (y - b) % SIDE for j in range(SIDE) for b in range(SIDE)]
            + [c]
        )
    return lax.dynamic_index_in_dim(
        jnp.array(table, jnp.int32), lax.axis_index("dp"), keepdims=False
    )


def weight_block(held, t):
    half = SIDE // 2

    def pick(side, b, j):
        return held[side, 2 * b + j // half, j % half, t]

    rows = []
    for j in range(SIDE):
        for b in range(SIDE):
            rows += [pick(0, b, j), pick(1, j, b)]
    return jnp.concatenate(rows, axis=0)


class Stream:
    def __init__(self, refs, held, sems, core, take):
        self.refs, self.held, self.sems = refs, held, sems
        self.core, self.take = core, take

    def start(self):
        sides, count, _, blocks = self.held.shape[:4]
        for n in range(blocks // self.take):
            span = pl.ds(n * self.take, self.take)
            for a, ref in enumerate(self.refs):
                side = 0 if sides == 1 else self.core if a < count else 1 - self.core
                pltpu.make_async_copy(
                    ref.at[:, span], self.held.at[side, a % count, :, span], self.sems.at[n]
                ).start()

    def wait(self, n):
        span = pl.ds(n * self.take, self.take)
        part = self.held.at[:, :, :, span]
        pltpu.make_async_copy(part, part, self.sems.at[n]).wait()


def project(mine, theirs, weights, place):
    rows, width = mine.shape
    half, blocks, depth, cols = weights[0].shape
    pair = 2
    count = len(weights)
    chips = width // LANE

    def kernel(place_ref, m_ref, t_ref, *refs):
        w_refs, a_ref, z_ref, raw, h, held, ready, sems = refs[:count], *refs[count:]
        copies = [
            pltpu.make_async_copy(ref, raw.at[pl.ds(n * rows, rows)], ready.at[n])
            for n, ref in enumerate((m_ref, t_ref))
        ]
        for copy in copies:
            copy.start()
        core = place_ref[chips]
        stream = Stream(w_refs, held, sems, core, TAKE)
        stream.start()
        for copy in copies:
            copy.wait()

        def line_up(c):
            parts = []
            for b in range(SIDE):
                for j in range(SIDE):
                    m = j * SIDE + b if c == 0 else b * SIDE + j
                    at = pl.multiple_of(place_ref[m] * LANE, LANE)
                    parts.append(raw[:, pl.ds(at, LANE)][:, c * depth : (c + 1) * depth])
            for n in range(0, chips, 2):
                h[:, n * depth : (n + 2) * depth] = jnp.concatenate(parts[n : n + 2], axis=1)

        for c in range(2):
            pl.when(core == c)(lambda c=c: line_up(c))
        for n in range(blocks // pair):
            if n * pair % TAKE == 0:
                stream.wait(n * pair // TAKE)
            w = jnp.concatenate(
                [
                    jnp.concatenate(
                        [held[0, a, i, n * pair + k] for a in range(count) for i in range(half)],
                        axis=0,
                    )
                    for k in range(pair)
                ],
                axis=1,
            )
            r = dot(h[...], w, NN)
            for k in range(pair):
                v = r[:, k * cols : (k + 1) * cols]
                a_ref[n * pair + k] = v[:rows]
                z_ref[n * pair + k] = v[rows:]

    return pl.pallas_call(
        kernel,
        in_specs=[pl.BlockSpec(memory_space=pltpu.SMEM)]
        + [pl.BlockSpec(memory_space=pl.ANY)] * (2 + count),
        out_specs=[pl.BlockSpec(memory_space=pltpu.VMEM)] * 2,
        scratch_shapes=[
            pltpu.VMEM((2 * rows, width), BF16),
            pltpu.VMEM((2 * rows, width // 2), BF16),
            pltpu.VMEM((1, count, half, blocks, depth, cols), BF16),
            pltpu.SemaphoreType.DMA((2,)),
            pltpu.SemaphoreType.DMA((blocks // TAKE,)),
        ],
        out_shape=[jax.ShapeDtypeStruct((blocks, rows, cols), F32)] * 2,
        compiler_params=params(32),
        cost_estimate=pl.CostEstimate(
            flops=2 * rows * width * blocks * cols,
            bytes_accessed=width * blocks * cols,
            transcendentals=0,
        ),
        name="project",
    )(place, mine, theirs, *weights)


def soft(scores, scale, total):
    peak = jnp.max(scores, axis=1, keepdims=True)
    e = jnp.exp2((scores - peak) * scale)
    return e * (total / jnp.sum(e, axis=1, keepdims=True))


def teacher_probs(teacher, seqs):
    blocks, rows, width = teacher.shape
    toks = rows // seqs
    length = blocks * toks
    heads = width // TH
    step = 256
    t4 = teacher.reshape(blocks, seqs, toks, width)

    def kernel(t_ref, o_ref):
        i = pl.program_id(2)
        part = step // toks
        t = t_ref[...].reshape(length, TH)
        q = t_ref[pl.ds(i * part, part)].reshape(step, TH)
        o_ref[0, 0] = soft(dot(q, t, NT), LOG2E / math.sqrt(TH), float(length))

    return pl.pallas_call(
        kernel,
        grid=(seqs, heads, length // step),
        in_specs=[
            pl.BlockSpec((blocks, None, toks, TH), lambda s, h, i: (0, s, 0, h))
        ],
        out_specs=pl.BlockSpec((1, 1, step, length), lambda s, h, i: (s, h, i, 0)),
        out_shape=jax.ShapeDtypeStruct((seqs, heads, length, length), F32),
        compiler_params=params(40),
        cost_estimate=pl.CostEstimate(
            flops=2 * seqs * heads * length * length * TH,
            bytes_accessed=4 * seqs * heads * length * length,
            transcendentals=seqs * heads * length * length,
        ),
        name="teacher_probs",
    )(t4)


def head_grads(student, probs):
    seqs = probs.shape[0]
    blocks, both, cols = student.shape
    toks = both // seqs
    length = blocks * toks
    heads = cols // SH
    step = 512
    part = step // toks
    last = length // step - 1

    def kernel(s_ref, p_ref, o_ref, b_ref, rows, trans):
        i = pl.program_id(1)
        s = s_ref[...].reshape(length, cols)
        q = s_ref[pl.ds(i * part, part)].reshape(step, cols)
        lane = lax.broadcasted_iota(jnp.int32, (step, cols), 1) // SH
        here = jnp.zeros((step, cols), F32)
        across = jnp.zeros((cols, length), F32)
        for h in range(heads):
            qh = jnp.where(lane == h, q, jnp.zeros_like(q))
            p = soft(dot(qh, s, NT), LOG2E / math.sqrt(SH), float(length))
            g = (p - p_ref[0, h]).astype(BF16)
            here = jnp.where(lane == h, dot(g, s, NN), here)
            across = across + dot(qh, g, TN)
        rows[pl.ds(i * step, step)] = here

        @pl.when(i == 0)
        def _():
            trans[...] = across

        @pl.when(i > 0)
        def _():
            trans[...] += across

        @pl.when(i == last)
        def _():
            grad = ((rows[...] + trans[...].T) * (1.0 / math.sqrt(SH))).astype(BF16)
            o_ref[...] = grad.reshape(blocks, toks, cols)
            total = jnp.sum(grad.astype(F32), axis=0, keepdims=True)
            b_ref[...] = jnp.where(pl.program_id(0) == 0, total, b_ref[...] + total)

    grads, total = pl.pallas_call(
        kernel,
        grid=(seqs, length // step),
        in_specs=[
            pl.BlockSpec((blocks, None, toks, cols), lambda s, i: (0, s, 0, 0)),
            pl.BlockSpec((1, heads, step, length), lambda s, i: (s, 0, i, 0)),
        ],
        out_specs=[
            pl.BlockSpec((blocks, None, toks, cols), lambda s, i: (0, s, 0, 0)),
            pl.BlockSpec((1, cols), lambda s, i: (0, 0)),
        ],
        out_shape=[
            jax.ShapeDtypeStruct((blocks, seqs, toks, cols), BF16),
            jax.ShapeDtypeStruct((1, cols), F32),
        ],
        scratch_shapes=[pltpu.VMEM((length, cols), F32), pltpu.VMEM((cols, length), F32)],
        compiler_params=params(58),
        cost_estimate=pl.CostEstimate(
            flops=6 * seqs * heads * length * length * cols,
            bytes_accessed=4 * seqs * heads * length * length,
            transcendentals=seqs * heads * length * length,
        ),
        name="head_grads",
    )(student.reshape(blocks, seqs, toks, cols), probs)
    return grads.reshape(student.shape), total


def hidden_grads(grads, weights, place):
    blocks, rows, cols = grads.shape
    half, _, depth, _ = weights[0].shape
    count = len(weights)
    width = count * half * depth
    pair = 2
    chips = width // LANE

    def kernel(place_ref, g_ref, *refs):
        w_refs, o_ref, acc, held, sems = refs[:count], *refs[count:]
        stream = Stream(w_refs, held, sems, place_ref[chips], TAKE)
        stream.start()
        for n in range(blocks // pair):
            if n * pair % TAKE == 0:
                stream.wait(n * pair // TAKE)
            w = jnp.concatenate(
                [weight_block(held, n * pair + k) for k in range(pair)], axis=1
            )
            g = jnp.concatenate([g_ref[n * pair + k] for k in range(pair)], axis=1)
            r = dot(g, w, NT)
            if n == 0:
                acc[...] = r
            else:
                acc[...] += r
        for m in range(chips):
            at = pl.multiple_of(place_ref[m] * LANE, LANE)
            o_ref[:, pl.ds(at, LANE)] = acc[:, m * LANE : (m + 1) * LANE].astype(BF16)

    return pl.pallas_call(
        kernel,
        in_specs=[
            pl.BlockSpec(memory_space=pltpu.SMEM),
            pl.BlockSpec(memory_space=pltpu.VMEM),
        ]
        + [pl.BlockSpec(memory_space=pl.ANY)] * count,
        out_specs=pl.BlockSpec(memory_space=pltpu.VMEM),
        scratch_shapes=[
            pltpu.VMEM((rows, width), F32),
            pltpu.VMEM((2, count // 2, half, blocks, depth, cols), BF16),
            pltpu.SemaphoreType.DMA((blocks // TAKE,)),
        ],
        out_shape=jax.ShapeDtypeStruct((rows, width), BF16),
        compiler_params=params(32),
        cost_estimate=pl.CostEstimate(
            flops=2 * rows * width * blocks * cols,
            bytes_accessed=2 * width * blocks * cols,
            transcendentals=0,
        ),
        name="hidden_grads",
    )(place, grads, *weights)


def sum_over(x, axis):
    size = lax.axis_size(axis)
    reach = 1
    while reach < size:
        x = x + lax.ppermute(x, axis, [(i, i ^ reach) for i in range(size)])
        reach *= 2
    return x


def exchange(x):
    return lax.all_to_all(x, "tok", split_axis=0, concat_axis=0, tiled=True)


def body(student_hidden, teacher_values, value_weight, value_bias):
    seqs, toks, width = student_hidden.shape
    groups, parts = lax.axis_size("dp"), lax.axis_size("tok")
    depth = width // groups

    group = lax.axis_index("dp").astype(jnp.int32)[None]
    piece = copies_of_piece(value_weight, value_bias, group, depth, parts)
    pieces = exchange(piece)
    bias = pieces[:, depth : depth + 1]

    columns = split_columns(teacher_values.reshape(seqs * toks, -1), parts)
    teacher = exchange(columns)
    weights = gather_weight(pieces[:, :depth])
    probs = teacher_probs(teacher, seqs)

    place = blocks_of()
    rows = student_hidden.reshape(seqs * toks, width)
    other_rows = swap_cores([rows])[0]
    swapped = swap_cores(weights[:EARLY])
    swapped += swap_cores(weights[EARLY : EARLY + 1])
    kept, sent = project(rows, other_rows, weights, place)
    got = swap_cores([sent])[0]
    values = (kept + got + bias.astype(F32)).astype(BF16)
    values = exchange(values)
    weights = weights + swapped + swap_cores(weights[EARLY + 1 :])
    grads, total = head_grads(values, probs)
    grads = exchange(grads)
    hidden_grad = hidden_grads(grads, weights, place).reshape(student_hidden.shape)
    tokens = seqs * toks * parts * groups
    bias_grad = sum_over(total, "dp")[0] / math.sqrt(tokens)
    return (hidden_grad, bias_grad)


def solution(mesh):
    placed = (P("dp", "tok", None), P("dp", "tok", None), P(None, "tok"), P(None, "tok"))
    return jax.shard_map(
        body,
        mesh=mesh,
        in_specs=placed,
        out_specs=(P("dp", "tok", None), P("tok")),
        check_vma=False,
    )
```
